32 devices in a mesh: vv: 4 (over y, core), oo: 8 (over z, x).
Axes of the slice: x: 2, y: 2, z: 4, core: 2. Of those that a mesh axis runs over, the one named last changes fastest.
Arguments:
- integrals: bfloat16 [1024, 256], P('vv', 'oo'), may hold values from -0.375 to 0.375
- amplitudes: bfloat16 [256, 4096], P('vv', 'oo'), may hold values from -6 to 6
- occ_energy: float32 [64], replicated, may hold values from -2 to -0.3
- vir_energy: float32 [32], replicated, may hold values from 0.1 to 3
Outputs:
- update: bfloat16 [1024, 4096], P('vv', 'oo')
The draws below stay inside these ranges and needn't reach their ends.
All inputs are finite; a program needn't handle non-finite values.
Results may differ from the reference program's by a relative error of at most 0.0085.
Values may be sent and summed in bfloat16 or wider, within the bound.
No kernel may reach another device: no remote copies, remote signals or barrier semaphores. Data moves between devices by JAX's collectives and lax.ppermute only.
A program may use at most 64 MiB of HBM per device.

```python
import jax
import jax.numpy as jnp
from jax import lax

CD = 256
VW = 32
OW = 64


def block_scale(key, extent, split, smallest, high):
    factor_of, own = 1.0, jax.random.fold_in(key, 6)
    for dim, blocks in split:
        steps = jnp.exp(jax.random.uniform(jax.random.fold_in(own, dim), (blocks,), jnp.float32, smallest / len(split), high / len(split)))
        factor_of = factor_of * jnp.repeat(steps, extent[dim] // blocks).reshape([-1 if axis == dim else 1 for axis in range(len(extent))])
    return factor_of


def bell_draw(stream_key, shape, deviation, most, shards=(), held_as=jnp.bfloat16):
    entries = jax.random.normal(stream_key, shape, jnp.float32) * deviation
    if len(shards) > 0:
        entries = block_scale(stream_key, shape, shards, -0.22, 0.18) * entries
    return jnp.clip(entries, min=-most, max=most).astype(held_as)


def setup_inputs(seed: int = 0) -> dict:
    splits = jax.random.split(jax.random.key(seed), 5)
    integrals = bell_draw(splits[0], (VW * VW, CD), CD ** -0.5, 0.375, ((0, 4), (1, 8)))
    amplitudes = bell_draw(splits[1], (CD, OW * OW), 1.0, 6.0, ((0, 4), (1, 8)))
    occ_energy = jnp.clip(jax.random.uniform(splits[2], (OW,), jnp.float32, -2.0, -0.3), -2.0, -0.3)
    vir_energy = jnp.clip(jax.random.uniform(splits[3], (VW,), jnp.float32, 0.1, 3.0), 0.1, 3.0)
    return dict(integrals=integrals, amplitudes=amplitudes, occ_energy=occ_energy, vir_energy=vir_energy)


def reference(integrals, amplitudes, occ_energy, vir_energy):
    cube = integrals.reshape(VW, VW, CD)
    flipped = jnp.transpose(cube, (1, 0, 2))
    amp_mirror = jnp.transpose(amplitudes.reshape(CD, OW, OW), (0, 2, 1)).reshape(CD, OW * OW)
    pair_occ = (occ_energy[:, None] + occ_energy[None, :]).reshape(OW * OW)

    def one_row(index):
        direct = jnp.dot(cube[index], amplitudes, preferred_element_type=jnp.float32).astype(jnp.bfloat16)
        mirror = jnp.dot(flipped[index], amp_mirror, preferred_element_type=jnp.float32).astype(jnp.bfloat16)
        denom = pair_occ[None, :] - vir_energy[index] - vir_energy[:, None]
        total = direct.astype(jnp.float32) + mirror.astype(jnp.float32)
        return (total / denom).astype(jnp.bfloat16)

    rows = lax.map(one_row, jnp.arange(VW, dtype=jnp.int32))
    return rows.reshape(VW * VW, OW * OW)
```

```python
import functools

import jax
import jax.numpy as jnp
from jax import lax
from jax.experimental import pallas as pl
from jax.experimental.pallas import tpu as pltpu
from jax.sharding import PartitionSpec as P

LANES = 128
F32 = jnp.float32
BF16 = jnp.bfloat16
VMEM = pltpu.MemorySpace.VMEM


def one_hot(rows, source):
    n = source.shape[1]
    pick = lax.broadcasted_iota(jnp.int32, (rows, n), 0) == source
    return jnp.where(pick, 1.0, 0.0).astype(BF16)


def columns(n):
    return lax.broadcasted_iota(jnp.int32, (1, n), 1)


def pack_kernel(occ_all, t_ref, v_ref, out_ref):
    parts, rows, lanes = out_ref.shape
    depth, cols = t_ref.shape
    own = cols // occ_all
    square = own * own
    col = columns(cols)
    source = (col % square // own) * occ_all + (col // square) * own + col % own
    moved = jnp.dot(t_ref[...], one_hot(cols, source), preferred_element_type=F32)
    fold = lanes // square
    high = depth // fold
    for part in range(parts):
        piece = [
            moved[h * high : (h + 1) * high, part * square : (part + 1) * square]
            for h in range(fold)
        ]
        out_ref[part, :high, :] = jnp.concatenate(piece, axis=1).astype(BF16)
    deep = v_ref.shape[0]
    for chunk in range((rows - high) // deep):
        block = v_ref[:, chunk * lanes : (chunk + 1) * lanes]
        for part in range(parts):
            out_ref[part, high + chunk * deep : high + (chunk + 1) * deep, :] = block


def integral_columns(got_ref, high, deep):
    parts, rows, lanes = got_ref.shape
    return jnp.concatenate(
        [
            got_ref[:, high + c * deep : high + (c + 1) * deep, :].reshape(parts * deep, lanes)
            for c in range((rows - high) // deep)
        ],
        axis=1,
    )


def split_kernel(sizes, got_ref, send_ref, keep_ref):
    vir_parts, vir_own, occ_own, high, deep, kept = sizes
    parts, _, lanes = got_ref.shape
    square = occ_own * occ_own
    fold = lanes // square
    cols = parts * square
    occ_all = parts * occ_own
    packed = got_ref[:, :high, :].astype(F32)
    halves = [
        jnp.concatenate(
            [packed[part, :, h * square : (h + 1) * square] for part in range(parts)], axis=1
        )
        for h in range(fold)
    ]
    amps = jnp.concatenate(halves, axis=0).astype(BF16)
    col = columns(cols)
    source = (col % occ_all // occ_own) * square + (col % occ_own) * occ_own + col // occ_all
    amps = jnp.dot(amps, one_hot(cols, source), preferred_element_type=F32).astype(BF16)
    depth = amps.shape[0]
    chunks = cols // lanes
    for c in range(chunks):
        block = amps[:, c * lanes : (c + 1) * lanes]
        send_ref[c * depth : (c + 1) * depth, :] = block
        keep_ref[c * depth : (c + 1) * depth, :] = block
    me = lax.axis_index("vv")
    ints = integral_columns(got_ref, high, deep)
    total, rows = ints.shape
    area = vir_own * vir_own
    col = columns(rows)
    owner = jnp.bitwise_xor(col // area, me)
    source = (col % vir_own) * (vir_parts * vir_own) + owner * vir_own + col % area // vir_own
    ints = jnp.dot(ints, one_hot(rows, source), preferred_element_type=F32).astype(BF16)
    base = chunks * depth
    for c in range(kept):
        keep_ref[base + c * total : base + (c + 1) * total, :] = ints[:, c * lanes : (c + 1) * lanes]
    first = rows // lanes - (send_ref.shape[0] - base) // total
    for c in range(first, rows // lanes):
        at = base + (c - first) * total
        send_ref[at : at + total, :] = ints[:, c * lanes : (c + 1) * lanes]


def direct_kernel(sizes, *refs):
    vir_parts, vir_own, occ_own, high, deep, width = sizes
    got_ref, occ_ref, row_ref, *amp_refs, lad_ref, den_ref, sel_ref, all_ref = refs
    me = lax.axis_index("vv")
    depth = amp_refs[0].shape[0]
    for rel, ref in enumerate(amp_refs):
        at = pl.multiple_of(jnp.bitwise_xor(me, rel) * depth, depth)
        all_ref[pl.ds(at, depth), :] = ref[...]
    ints = integral_columns(got_ref, high, deep)
    lad_ref[...] = lax.dot_general(
        ints, all_ref[...], (((0,), (0,)), ((), ())), preferred_element_type=F32
    ).astype(BF16)
    den_ref[...] = occ_ref[...] - row_ref[:, :1] - row_ref[:, 1:]
    rows, n = sel_ref.shape
    area = vir_own * vir_own
    vir_all = vir_parts * vir_own
    row = lax.broadcasted_iota(jnp.int32, (rows, 1), 0)
    rel = jnp.bitwise_xor(row % vir_all // vir_own, me)
    source = rel * width + (rel % (width // area)) * area + row // vir_all * vir_own + row % vir_own
    pick = lax.broadcasted_iota(jnp.int32, (rows, n), 1) == source
    sel_ref[...] = jnp.where(pick, 1.0, 0.0).astype(BF16)


def mirror_kernel(sizes, *refs):
    depth, total, width = sizes
    lad_ref, den_ref, sel_ref, *got_refs, out_ref, all_ref = refs
    me = lax.axis_index("vv")
    rows, cols = out_ref.shape
    chunks = cols // LANES
    for rel, ref in enumerate(got_refs):
        at = pl.multiple_of(jnp.bitwise_xor(me, rel) * depth, depth)
        for c in range(chunks):
            all_ref[pl.ds(at, depth), c * LANES : (c + 1) * LANES] = ref[c * depth : (c + 1) * depth, :]
    base = chunks * depth
    ints = jnp.concatenate(
        [
            ref[base + c * total : base + (c + 1) * total, :]
            for ref in got_refs
            for c in range(width // LANES)
        ],
        axis=1,
    )
    rows_mirrored = lax.dot_general(
        sel_ref[...], ints, (((1,), (1,)), ((), ())), preferred_element_type=F32
    ).astype(BF16)
    mirrored = jnp.dot(rows_mirrored, all_ref[...], preferred_element_type=F32).astype(BF16)
    total_sum = lad_ref[...].astype(F32) + mirrored.astype(F32)
    out_ref[...] = (total_sum / den_ref[...]).astype(BF16)


def call(kernel, outs, args, scratch=(), flops=0):
    outs = tuple(outs)
    moved = sum(x.size * x.dtype.itemsize for x in (*args, *outs))
    result = pl.pallas_call(
        kernel,
        out_shape=outs,
        in_specs=[pl.BlockSpec(memory_space=VMEM)] * len(args),
        out_specs=tuple(pl.BlockSpec(memory_space=VMEM) for _ in outs),
        scratch_shapes=list(scratch),
        cost_estimate=pl.CostEstimate(flops=flops, bytes_accessed=moved, transcendentals=0),
    )(*args)
    return result


def on_device(integrals, amplitudes, occ_energy, vir_energy):
    vir_parts, occ_parts = lax.axis_size("vv"), lax.axis_size("oo")
    vir_all, occ_all = vir_energy.shape[0], occ_energy.shape[0]
    vir_own, occ_own = vir_all // vir_parts, occ_all // occ_parts
    depth, cols = amplitudes.shape
    rows, deep = integrals.shape
    total = deep * occ_parts
    high = depth * occ_own * occ_own // LANES
    area = vir_own * vir_own

    def swap(x, step):
        return lax.ppermute(x, "vv", [(k, k ^ step) for k in range(vir_parts)])

    shape = (occ_parts, high + rows // LANES * deep, LANES)
    (packed,) = call(
        functools.partial(pack_kernel, occ_all),
        [jax.ShapeDtypeStruct(shape, BF16)],
        (amplitudes, integrals.T),
        flops=2 * depth * cols * cols,
    )
    got = lax.all_to_all(packed, "oo", 0, 0, tiled=True)

    step = vir_parts // 2
    lanes = rows
    halves = step * area % LANES == 0
    send_lanes = lanes // 2 if halves else lanes
    amp_rows = cols // LANES * depth
    send, keep = call(
        functools.partial(
            split_kernel, (vir_parts, vir_own, occ_own, high, deep, send_lanes // LANES)
        ),
        [jax.ShapeDtypeStruct((amp_rows + send_lanes // LANES * total, LANES), BF16)] * 2,
        (got,),
        flops=2 * depth * cols * cols + 2 * total * rows * rows,
    )
    held = {0: (send, keep)}
    direct = {0: amplitudes}
    lanes = send_lanes
    while step:
        direct |= {k ^ step: swap(x, step) for k, x in direct.items()}
        arrived = {k: x for k, (_, x) in held.items()}
        arrived |= {k ^ step: swap(x, step) for k, (x, _) in held.items()}
        step //= 2
        if step and step * area % LANES == 0:
            lanes //= 2
            cut = amp_rows + lanes // LANES * total
            held = {
                k: (jnp.concatenate([x[:amp_rows], x[cut:]]), x[:cut]) for k, x in arrived.items()
            }
        else:
            held = {k: (x, x) for k, x in arrived.items()}
    order = range(vir_parts)

    vir_mine = lax.dynamic_slice_in_dim(vir_energy, lax.axis_index("vv") * vir_own, vir_own, 0)
    occ_mine = lax.dynamic_slice_in_dim(occ_energy, lax.axis_index("oo") * occ_own, occ_own, 0)
    occ_pair = (occ_mine[:, None] + occ_energy[None, :]).reshape(1, cols)
    vir_pair = jnp.stack(
        [
            jnp.broadcast_to(vir_mine[:, None], (vir_own, vir_all)),
            jnp.broadcast_to(vir_energy[None, :], (vir_own, vir_all)),
        ],
        axis=-1,
    ).reshape(rows, 2)
    ladder, denom, select = call(
        functools.partial(direct_kernel, (vir_parts, vir_own, occ_own, high, deep, lanes)),
        [
            jax.ShapeDtypeStruct((rows, cols), BF16),
            jax.ShapeDtypeStruct((rows, cols), F32),
            jax.ShapeDtypeStruct((rows, vir_parts * lanes), BF16),
        ],
        (got, occ_pair, vir_pair, *(direct[k] for k in order)),
        scratch=[pltpu.VMEM((total, cols), BF16)],
        flops=2 * rows * total * cols,
    )
    (update,) = call(
        functools.partial(mirror_kernel, (depth, total, lanes)),
        [jax.ShapeDtypeStruct((rows, cols), BF16)],
        (ladder, denom, select, *(arrived[k] for k in order)),
        scratch=[pltpu.VMEM((total, cols), BF16)],
        flops=2 * rows * total * cols * 2,
    )
    return update


def solution(mesh):
    placed = (P("vv", "oo"), P("vv", "oo"), P(), P())
    return jax.shard_map(
        on_device, mesh=mesh, in_specs=placed, out_specs=P("vv", "oo"), check_vma=False
    )
```

```python
import functools

import jax
import jax.numpy as jnp
from jax import lax
from jax.experimental import pallas as pl
from jax.experimental.pallas import tpu as pltpu
from jax.sharding import PartitionSpec as P

LANES = 128
LEAST, MOST = 8 << 20, 60 << 20
F32 = jnp.float32
BF16 = jnp.bfloat16
VMEM = pltpu.MemorySpace.VMEM


def one_hot(rows, source):
    n = source.shape[1]
    pick = lax.broadcasted_iota(jnp.int32, (rows, n), 0) == source
    return jnp.where(pick, 1.0, 0.0).astype(BF16)


def columns(n):
    return lax.broadcasted_iota(jnp.int32, (1, n), 1)


def square_eye(n):
    return lax.broadcasted_iota(jnp.int32, (n, n), 0) == lax.broadcasted_iota(jnp.int32, (n, n), 1)


def pick_sum(values, where, axis):
    return jnp.sum(jnp.where(where, values, 0.0), axis=axis, keepdims=True)


def pack_kernel(occ_all, t_ref, v_ref, out_ref):
    parts, rows, lanes = out_ref.shape
    depth, cols = t_ref.shape
    own = cols // occ_all
    square = own * own
    col = columns(cols)
    source = (col % square // own) * occ_all + (col // square) * own + col % own
    moved = jnp.dot(t_ref[...], one_hot(cols, source), preferred_element_type=F32)
    fold = lanes // square
    high = depth // fold
    for part in range(parts):
        piece = [
            moved[h * high : (h + 1) * high, part * square : (part + 1) * square]
            for h in range(fold)
        ]
        out_ref[part, :high, :] = jnp.concatenate(piece, axis=1).astype(BF16)
    deep = v_ref.shape[0]
    for chunk in range((rows - high) // deep):
        block = v_ref[:, chunk * lanes : (chunk + 1) * lanes]
        for part in range(parts):
            out_ref[part, high + chunk * deep : high + (chunk + 1) * deep, :] = block


def integral_columns(got_ref, high, deep):
    parts, rows, lanes = got_ref.shape
    return jnp.concatenate(
        [
            got_ref[:, high + c * deep : high + (c + 1) * deep, :].reshape(parts * deep, lanes)
            for c in range((rows - high) // deep)
        ],
        axis=1,
    )


def split_kernel(sizes, got_ref, send_ref, keep_ref):
    vir_parts, vir_own, occ_own, high, deep, kept = sizes
    parts, _, lanes = got_ref.shape
    square = occ_own * occ_own
    fold = lanes // square
    cols = parts * square
    occ_all = parts * occ_own
    packed = got_ref[:, :high, :].astype(F32)
    halves = [
        jnp.concatenate(
            [packed[part, :, h * square : (h + 1) * square] for part in range(parts)], axis=1
        )
        for h in range(fold)
    ]
    amps = jnp.concatenate(halves, axis=0).astype(BF16)
    col = columns(cols)
    source = (col % occ_all // occ_own) * square + (col % occ_own) * occ_own + col // occ_all
    amps = jnp.dot(amps, one_hot(cols, source), preferred_element_type=F32).astype(BF16)
    depth = amps.shape[0]
    chunks = cols // lanes
    for c in range(chunks):
        block = amps[:, c * lanes : (c + 1) * lanes]
        send_ref[c * depth : (c + 1) * depth, :] = block
        keep_ref[c * depth : (c + 1) * depth, :] = block
    me = lax.axis_index("vv")
    ints = integral_columns(got_ref, high, deep)
    total, rows = ints.shape
    area = vir_own * vir_own
    col = columns(rows)
    owner = jnp.bitwise_xor(col // area, me)
    source = (col % vir_own) * (vir_parts * vir_own) + owner * vir_own + col % area // vir_own
    ints = jnp.dot(ints, one_hot(rows, source), preferred_element_type=F32).astype(BF16)
    base = chunks * depth
    for c in range(kept):
        keep_ref[base + c * total : base + (c + 1) * total, :] = ints[:, c * lanes : (c + 1) * lanes]
    first = rows // lanes - (send_ref.shape[0] - base) // total
    for c in range(first, rows // lanes):
        at = base + (c - first) * total
        send_ref[at : at + total, :] = ints[:, c * lanes : (c + 1) * lanes]


def direct_kernel(sizes, *refs):
    vir_parts, vir_own, occ_own, high, deep, width = sizes
    got_ref, occ_ref, vir_ref, *amp_refs, lad_ref, den_ref, sel_ref, all_ref = refs
    me = lax.axis_index("vv")
    depth = amp_refs[0].shape[0]
    for rel, ref in enumerate(amp_refs):
        at = pl.multiple_of(jnp.bitwise_xor(me, rel) * depth, depth)
        all_ref[pl.ds(at, depth), :] = ref[...]
    ints = integral_columns(got_ref, high, deep)
    lad_ref[...] = lax.dot_general(
        ints, all_ref[...], (((0,), (0,)), ((), ())), preferred_element_type=F32
    ).astype(BF16)
    rows, cols = den_ref.shape
    vir_all, occ_all = vir_parts * vir_own, occ_ref.shape[1]
    occ = occ_ref[...]
    occ_column = pick_sum(occ, square_eye(occ_all), 1)
    mine = lax.axis_index("oo") * occ_own + columns(cols) // occ_all
    occ_mine = pick_sum(occ_column, lax.broadcasted_iota(jnp.int32, (occ_all, cols), 0) == mine, 0)
    occ_pair = occ_mine + jnp.concatenate([occ] * occ_own, axis=1)
    lane = lax.broadcasted_iota(jnp.int32, (rows, vir_all), 1)
    row = lax.broadcasted_iota(jnp.int32, (rows, 1), 0)
    vir = vir_ref[...]
    vir_mine = pick_sum(vir, lane == me * vir_own + row // vir_all, 1)
    vir_other = pick_sum(vir, lane == row % vir_all, 1)
    den_ref[...] = occ_pair - vir_mine - vir_other
    n = sel_ref.shape[1]
    area = vir_own * vir_own
    rel = jnp.bitwise_xor(row % vir_all // vir_own, me)
    source = rel * width + (rel % (width // area)) * area + row // vir_all * vir_own + row % vir_own
    pick = lax.broadcasted_iota(jnp.int32, (rows, n), 1) == source
    sel_ref[...] = jnp.where(pick, 1.0, 0.0).astype(BF16)


def mirror_kernel(sizes, *refs):
    depth, total, width = sizes
    lad_ref, den_ref, sel_ref, *got_refs, out_ref, all_ref = refs
    me = lax.axis_index("vv")
    rows, cols = out_ref.shape
    chunks = cols // LANES
    for rel, ref in enumerate(got_refs):
        at = pl.multiple_of(jnp.bitwise_xor(me, rel) * depth, depth)
        for c in range(chunks):
            all_ref[pl.ds(at, depth), c * LANES : (c + 1) * LANES] = ref[c * depth : (c + 1) * depth, :]
    base = chunks * depth
    ints = jnp.concatenate(
        [
            ref[base + c * total : base + (c + 1) * total, :]
            for ref in got_refs
            for c in range(width // LANES)
        ],
        axis=1,
    )
    rows_mirrored = lax.dot_general(
        sel_ref[...], ints, (((1,), (1,)), ((), ())), preferred_element_type=F32
    ).astype(BF16)
    mirrored = jnp.dot(rows_mirrored, all_ref[...], preferred_element_type=F32).astype(BF16)
    total_sum = lad_ref[...].astype(F32) + mirrored.astype(F32)
    out_ref[...] = (total_sum / den_ref[...]).astype(BF16)


def call(kernel, outs, args, scratch=(), flops=0):
    outs = tuple(outs)
    moved = sum(x.size * x.dtype.itemsize for x in (*args, *outs))
    result = pl.pallas_call(
        kernel,
        out_shape=outs,
        in_specs=[pl.BlockSpec(memory_space=VMEM)] * len(args),
        out_specs=tuple(pl.BlockSpec(memory_space=VMEM) for _ in outs),
        scratch_shapes=list(scratch),
        compiler_params=pltpu.CompilerParams(vmem_limit_bytes=min(MOST, LEAST + 3 * moved)),
        cost_estimate=pl.CostEstimate(flops=flops, bytes_accessed=moved, transcendentals=0),
    )(*args)
    return result


def on_device(integrals, amplitudes, occ_energy, vir_energy):
    vir_parts, occ_parts = lax.axis_size("vv"), lax.axis_size("oo")
    vir_all, occ_all = vir_energy.shape[0], occ_energy.shape[0]
    vir_own, occ_own = vir_all // vir_parts, occ_all // occ_parts
    depth, cols = amplitudes.shape
    rows, deep = integrals.shape
    total = deep * occ_parts
    high = depth * occ_own * occ_own // LANES
    area = vir_own * vir_own

    def swap(x, step):
        return lax.ppermute(x, "vv", [(k, k ^ step) for k in range(vir_parts)])

    shape = (occ_parts, high + rows // LANES * deep, LANES)
    (packed,) = call(
        functools.partial(pack_kernel, occ_all),
        [jax.ShapeDtypeStruct(shape, BF16)],
        (amplitudes, integrals.T),
        flops=2 * depth * cols * cols,
    )
    got = lax.all_to_all(packed, "oo", 0, 0, tiled=True)

    step = vir_parts // 2
    lanes = rows
    halves = step * area % LANES == 0
    send_lanes = lanes // 2 if halves else lanes
    amp_rows = cols // LANES * depth
    send, keep = call(
        functools.partial(
            split_kernel, (vir_parts, vir_own, occ_own, high, deep, send_lanes // LANES)
        ),
        [jax.ShapeDtypeStruct((amp_rows + send_lanes // LANES * total, LANES), BF16)] * 2,
        (got,),
        flops=2 * depth * cols * cols + 2 * total * rows * rows,
    )
    held = {0: (send, keep)}
    direct = {0: amplitudes}
    lanes = send_lanes
    while step:
        direct |= {k ^ step: swap(x, step) for k, x in direct.items()}
        arrived = {k: x for k, (_, x) in held.items()}
        arrived |= {k ^ step: swap(x, step) for k, (x, _) in held.items()}
        step //= 2
        if step and step * area % LANES == 0:
            lanes //= 2
            cut = amp_rows + lanes // LANES * total
            held = {
                k: (jnp.concatenate([x[:amp_rows], x[cut:]]), x[:cut]) for k, x in arrived.items()
            }
        else:
            held = {k: (x, x) for k, x in arrived.items()}
    order = range(vir_parts)

    ladder, denom, select = call(
        functools.partial(direct_kernel, (vir_parts, vir_own, occ_own, high, deep, lanes)),
        [
            jax.ShapeDtypeStruct((rows, cols), BF16),
            jax.ShapeDtypeStruct((rows, cols), F32),
            jax.ShapeDtypeStruct((rows, vir_parts * lanes), BF16),
        ],
        (got, occ_energy.reshape(1, occ_all), vir_energy.reshape(1, vir_all), *(direct[k] for k in order)),
        scratch=[pltpu.VMEM((total, cols), BF16)],
        flops=2 * rows * total * cols,
    )
    (update,) = call(
        functools.partial(mirror_kernel, (depth, total, lanes)),
        [jax.ShapeDtypeStruct((rows, cols), BF16)],
        (ladder, denom, select, *(arrived[k] for k in order)),
        scratch=[pltpu.VMEM((total, cols), BF16)],
        flops=2 * rows * total * cols * 2,
    )
    return update


def solution(mesh):
    placed = (P("vv", "oo"), P("vv", "oo"), P(), P())
    return jax.shard_map(
        on_device, mesh=mesh, in_specs=placed, out_specs=P("vv", "oo"), check_vma=False
    )
```

```python
import functools

import jax
import jax.numpy as jnp
from jax import lax
from jax.experimental import pallas as pl
from jax.experimental.pallas import tpu as pltpu
from jax.sharding import PartitionSpec as P


LANES = 128
LEAST, MOST = 8 << 20, 60 << 20
CHOOSE_FLOPS = 10**9
F32 = jnp.float32
BF16 = jnp.bfloat16
VMEM = pltpu.MemorySpace.VMEM


def one_hot(rows, source):
    n = source.shape[1]
    pick = lax.broadcasted_iota(jnp.int32, (rows, n), 0) == source
    return jnp.where(pick, 1.0, 0.0).astype(BF16)


def columns(n):
    return lax.broadcasted_iota(jnp.int32, (1, n), 1)


def square_eye(n):
    return lax.broadcasted_iota(jnp.int32, (n, n), 0) == lax.broadcasted_iota(jnp.int32, (n, n), 1)


def pick_sum(values, where, axis):
    return jnp.sum(jnp.where(where, values, 0.0), axis=axis, keepdims=True)


def pack_kernel(own, t_ref, v_ref, source_ref, out_ref):
    parts, rows, lanes = out_ref.shape
    depth, cols = t_ref.shape
    square = own * own
    moved = jnp.dot(t_ref[...], one_hot(cols, source_ref[...]), preferred_element_type=F32)
    fold = lanes // square
    high = depth // fold
    for part in range(parts):
        piece = [
            moved[h * high : (h + 1) * high, part * square : (part + 1) * square]
            for h in range(fold)
        ]
        out_ref[part, :high, :] = jnp.concatenate(piece, axis=1).astype(BF16)
    deep = v_ref.shape[0]
    for chunk in range((rows - high) // deep):
        block = v_ref[:, chunk * lanes : (chunk + 1) * lanes]
        for part in range(parts):
            out_ref[part, high + chunk * deep : high + (chunk + 1) * deep, :] = block


def integral_columns(got_ref, high, deep):
    parts, rows, lanes = got_ref.shape
    return jnp.concatenate(
        [
            got_ref[:, high + c * deep : high + (c + 1) * deep, :].reshape(parts * deep, lanes)
            for c in range((rows - high) // deep)
        ],
        axis=1,
    )


def split_kernel(sizes, got_ref, send_ref, keep_ref):
    vir_parts, vir_own, occ_own, high, deep, kept = sizes
    parts, _, lanes = got_ref.shape
    square = occ_own * occ_own
    fold = lanes // square
    cols = parts * square
    packed = got_ref[:, :high, :].astype(F32)
    halves = [
        jnp.concatenate(
            [packed[part, :, h * square : (h + 1) * square] for part in range(parts)], axis=1
        )
        for h in range(fold)
    ]
    amps = jnp.concatenate(halves, axis=0).astype(BF16)
    col, occ_all = columns(cols), parts * occ_own
    source = (col % occ_all // occ_own) * square + (col % occ_own) * occ_own + col // occ_all
    amps = jnp.dot(amps, one_hot(cols, source), preferred_element_type=F32).astype(BF16)
    depth = amps.shape[0]
    chunks = cols // lanes
    for c in range(chunks):
        block = amps[:, c * lanes : (c + 1) * lanes]
        send_ref[c * depth : (c + 1) * depth, :] = block
        keep_ref[c * depth : (c + 1) * depth, :] = block
    ints = integral_columns(got_ref, high, deep)
    total, rows = ints.shape
    col, area = columns(rows), vir_own * vir_own
    owner = jnp.bitwise_xor(col // area, lax.axis_index("vv"))
    source = (col % vir_own) * (vir_parts * vir_own) + owner * vir_own + col % area // vir_own
    ints = jnp.dot(ints, one_hot(rows, source), preferred_element_type=F32).astype(BF16)
    base = chunks * depth
    for c in range(kept):
        keep_ref[base + c * total : base + (c + 1) * total, :] = ints[:, c * lanes : (c + 1) * lanes]
    first = rows // lanes - (send_ref.shape[0] - base) // total
    for c in range(first, rows // lanes):
        at = base + (c - first) * total
        send_ref[at : at + total, :] = ints[:, c * lanes : (c + 1) * lanes]


def direct_kernel(sizes, *refs):
    vir_parts, vir_own, occ_own, high, deep, width = sizes
    got_ref, occ_ref, vir_ref, *amp_refs, lad_ref, den_ref, sel_ref, all_ref = refs
    me = lax.axis_index("vv")
    depth = amp_refs[0].shape[0]
    for rel, ref in enumerate(amp_refs):
        at = pl.multiple_of(jnp.bitwise_xor(me, rel) * depth, depth)
        all_ref[pl.ds(at, depth), :] = ref[...]
    ints = integral_columns(got_ref, high, deep)
    lad_ref[...] = lax.dot_general(
        ints, all_ref[...], (((0,), (0,)), ((), ())), preferred_element_type=F32
    ).astype(BF16)
    rows, cols = den_ref.shape
    vir_all, occ_all = vir_parts * vir_own, occ_ref.shape[1]
    occ = occ_ref[...]
    occ_column = pick_sum(occ, square_eye(occ_all), 1)
    mine = lax.axis_index("oo") * occ_own + columns(cols) // occ_all
    occ_mine = pick_sum(occ_column, lax.broadcasted_iota(jnp.int32, (occ_all, cols), 0) == mine, 0)
    occ_pair = occ_mine + jnp.concatenate([occ] * occ_own, axis=1)
    lane = lax.broadcasted_iota(jnp.int32, (rows, vir_all), 1)
    row = lax.broadcasted_iota(jnp.int32, (rows, 1), 0)
    vir = vir_ref[...]
    vir_mine = pick_sum(vir, lane == me * vir_own + row // vir_all, 1)
    vir_other = pick_sum(vir, lane == row % vir_all, 1)
    den_ref[...] = occ_pair - vir_mine - vir_other
    n, area = sel_ref.shape[1], vir_own * vir_own
    rel = jnp.bitwise_xor(row % vir_all // vir_own, me)
    source = rel * width + (rel % (width // area)) * area + row // vir_all * vir_own + row % vir_own
    pick = lax.broadcasted_iota(jnp.int32, (rows, n), 1) == source
    sel_ref[...] = jnp.where(pick, 1.0, 0.0).astype(BF16)


def choose_kernel(own, source_ref):
    cols = source_ref.shape[1]
    square, occ_all = own * own, cols // own
    col = columns(cols)
    source_ref[...] = (col % square // own) * occ_all + (col // square) * own + col % own


def mirror_kernel(sizes, *refs):
    depth, total, width = sizes
    lad_ref, den_ref, sel_ref, *got_refs, out_ref, all_ref = refs
    me = lax.axis_index("vv")
    _, cols = out_ref.shape
    chunks = cols // LANES
    for rel, ref in enumerate(got_refs):
        at = pl.multiple_of(jnp.bitwise_xor(me, rel) * depth, depth)
        for c in range(chunks):
            all_ref[pl.ds(at, depth), c * LANES : (c + 1) * LANES] = ref[c * depth : (c + 1) * depth, :]
    base = chunks * depth
    ints = jnp.concatenate(
        [
            ref[base + c * total : base + (c + 1) * total, :]
            for ref in got_refs
            for c in range(width // LANES)
        ],
        axis=1,
    )
    rows_mirrored = lax.dot_general(
        sel_ref[...], ints, (((1,), (1,)), ((), ())), preferred_element_type=F32
    ).astype(BF16)
    mirrored = jnp.dot(rows_mirrored, all_ref[...], preferred_element_type=F32).astype(BF16)
    total_sum = lad_ref[...].astype(F32) + mirrored.astype(F32)
    out_ref[...] = (total_sum / den_ref[...]).astype(BF16)


def call(kernel, outs, args, scratch=(), flops=0, space=VMEM):
    outs = tuple(outs)
    moved = sum(x.size * x.dtype.itemsize for x in (*args, *outs))
    result = pl.pallas_call(
        kernel,
        out_shape=outs,
        in_specs=[pl.BlockSpec(memory_space=space)] * len(args),
        out_specs=tuple(pl.BlockSpec(memory_space=VMEM) for _ in outs),
        scratch_shapes=list(scratch),
        compiler_params=pltpu.CompilerParams(vmem_limit_bytes=min(MOST, LEAST + 3 * moved)),
        cost_estimate=pl.CostEstimate(flops=flops, bytes_accessed=moved, transcendentals=0),
    )(*args)
    return result


def on_device(integrals, amplitudes, occ_energy, vir_energy):
    vir_parts, occ_parts = lax.axis_size("vv"), lax.axis_size("oo")
    vir_all, occ_all = vir_energy.shape[0], occ_energy.shape[0]
    vir_own, occ_own = vir_all // vir_parts, occ_all // occ_parts
    depth, cols = amplitudes.shape
    rows, deep = integrals.shape
    total = deep * occ_parts
    high = depth * occ_own * occ_own // LANES
    area = vir_own * vir_own

    def swap(x, step):
        return lax.ppermute(x, "vv", [(k, k ^ step) for k in range(vir_parts)])

    steps = [1 << bit for bit in reversed(range((vir_parts - 1).bit_length()))]
    widths = [s * area for s in steps if s * area % LANES == 0] or [rows]
    width = widths[-1]

    (source,) = call(
        functools.partial(choose_kernel, occ_own),
        [jax.ShapeDtypeStruct((1, cols), jnp.int32)],
        (),
        flops=CHOOSE_FLOPS,
    )

    shape = (occ_parts, high + rows // LANES * deep, LANES)
    (packed,) = call(
        functools.partial(pack_kernel, occ_own),
        [jax.ShapeDtypeStruct(shape, BF16)],
        (amplitudes, integrals.T, source),
        flops=2 * depth * cols * cols,
    )
    got = lax.all_to_all(packed, "oo", 0, 0, tiled=True)

    amp_rows = cols // LANES * depth
    send_shape = jax.ShapeDtypeStruct((amp_rows + widths[0] // LANES * total, LANES), BF16)
    send, keep = call(
        functools.partial(
            split_kernel, (vir_parts, vir_own, occ_own, high, deep, widths[0] // LANES)
        ),
        [send_shape] * 2,
        (got,),
        flops=2 * depth * cols * cols + 2 * total * rows * rows,
    )
    held = {0: (send, keep)}
    direct = {0: amplitudes}
    for at, step in enumerate(steps):
        direct |= {k ^ step: swap(x, step) for k, x in direct.items()}
        arrived = {k: x for k, (_, x) in held.items()}
        arrived |= {k ^ step: swap(x, step) for k, (x, _) in held.items()}
        if at + 1 < len(widths):
            cut = amp_rows + widths[at + 1] // LANES * total
            held = {
                k: (jnp.concatenate([x[:amp_rows], x[cut:]]), x[:cut]) for k, x in arrived.items()
            }
        else:
            held = {k: (x, x) for k, x in arrived.items()}
    order = range(vir_parts)

    ladder, denom, to_rows = call(
        functools.partial(direct_kernel, (vir_parts, vir_own, occ_own, high, deep, width)),
        [
            jax.ShapeDtypeStruct((rows, cols), BF16),
            jax.ShapeDtypeStruct((rows, cols), F32),
            jax.ShapeDtypeStruct((rows, vir_parts * width), BF16),
        ],
        (
            got,
            occ_energy.reshape(1, occ_all),
            vir_energy.reshape(1, vir_all),
            *(direct[k] for k in order),
        ),
        scratch=[pltpu.VMEM((total, cols), BF16)],
        flops=2 * rows * total * cols,
    )
    (update,) = call(
        functools.partial(mirror_kernel, (depth, total, width)),
        [jax.ShapeDtypeStruct((rows, cols), BF16)],
        (ladder, denom, to_rows, *(arrived[k] for k in order)),
        scratch=[pltpu.VMEM((total, cols), BF16)],
        flops=2 * rows * total * cols * 2,
    )
    return update


def solution(mesh):
    placed = (P("vv", "oo"), P("vv", "oo"), P(), P())
    return jax.shard_map(
        on_device, mesh=mesh, in_specs=placed, out_specs=P("vv", "oo"), check_vma=False
    )
```

```python
import functools

import jax
import jax.numpy as jnp
from jax import lax
from jax.experimental import pallas as pl
from jax.experimental.pallas import tpu as pltpu
from jax.sharding import PartitionSpec as P


LANES, STORES = 128, 2
LEAST, MOST = 8 << 20, 60 << 20
CHOOSE_FLOPS = 10**9
F32 = jnp.float32
BF16 = jnp.bfloat16
VMEM = pltpu.MemorySpace.VMEM


def one_hot(rows, source):
    n = source.shape[1]
    pick = lax.broadcasted_iota(jnp.int32, (rows, n), 0) == source
    return jnp.where(pick, 1.0, 0.0).astype(BF16)


def middle_out(n):
    half, chunk = n // 2, max(1, n // 4)
    up, down = list(range(half, n)), list(reversed(range(half)))
    order = []
    for at in range(0, max(len(up), len(down)), chunk):
        order += up[at : at + chunk] + down[at : at + chunk]
    return order


def places(n):
    order = middle_out(n)
    return [order.index(k) for k in range(n)]


def columns(n):
    return lax.broadcasted_iota(jnp.int32, (1, n), 1)


def square_eye(n):
    return lax.broadcasted_iota(jnp.int32, (n, n), 0) == lax.broadcasted_iota(jnp.int32, (n, n), 1)


def pick_sum(values, where, axis):
    return jnp.sum(jnp.where(where, values, 0.0), axis=axis, keepdims=True)


def pack_kernel(own, t_ref, v_ref, source_ref, out_ref):
    parts, rows, lanes = out_ref.shape
    depth, cols = t_ref.shape
    square = own * own
    moved = jnp.dot(t_ref[...], one_hot(cols, source_ref[...]), preferred_element_type=F32)
    fold = lanes // square
    high = depth // fold
    for at, part in enumerate(middle_out(parts)):
        piece = [
            moved[h * high : (h + 1) * high, part * square : (part + 1) * square]
            for h in range(fold)
        ]
        out_ref[at, :high, :] = jnp.concatenate(piece, axis=1).astype(BF16)
    deep = v_ref.shape[0]
    for chunk in range((rows - high) // deep):
        block = v_ref[:, chunk * lanes : (chunk + 1) * lanes]
        for part in range(parts):
            out_ref[part, high + chunk * deep : high + (chunk + 1) * deep, :] = block


def integral_columns(got_ref, high, deep):
    parts, rows, _ = got_ref.shape
    return jnp.concatenate(
        [
            jnp.concatenate(
                [got_ref[at, high + c * deep : high + (c + 1) * deep, :] for at in places(parts)],
                axis=0,
            )
            for c in range((rows - high) // deep)
        ],
        axis=1,
    )


def split_kernel(sizes, got_ref, send_ref, keep_ref):
    vir_parts, vir_own, occ_own, high, deep, kept = sizes
    parts, _, lanes = got_ref.shape
    square = occ_own * occ_own
    fold = lanes // square
    cols = parts * square
    packed = got_ref[:, :high, :].astype(F32)
    halves = [
        jnp.concatenate(
            [packed[at, :, h * square : (h + 1) * square] for at in places(parts)], axis=1
        )
        for h in range(fold)
    ]
    amps = jnp.concatenate(halves, axis=0).astype(BF16)
    col, occ_all = columns(cols), parts * occ_own
    source = (col % occ_all // occ_own) * square + (col % occ_own) * occ_own + col // occ_all
    amps = jnp.dot(amps, one_hot(cols, source), preferred_element_type=F32).astype(BF16)
    depth = amps.shape[0]
    chunks = cols // lanes
    for c in range(chunks):
        block = amps[:, c * lanes : (c + 1) * lanes]
        send_ref[c * depth : (c + 1) * depth, :] = block
        keep_ref[c * depth : (c + 1) * depth, :] = block
    ints = integral_columns(got_ref, high, deep)
    total, rows = ints.shape
    col, area = columns(rows), vir_own * vir_own
    owner = jnp.bitwise_xor(col // area, lax.axis_index("vv"))
    source = (col % vir_own) * (vir_parts * vir_own) + owner * vir_own + col % area // vir_own
    ints = jnp.dot(ints, one_hot(rows, source), preferred_element_type=F32).astype(BF16)
    base = chunks * depth
    for c in range(kept):
        keep_ref[base + c * total : base + (c + 1) * total, :] = ints[:, c * lanes : (c + 1) * lanes]
    first = rows // lanes - (send_ref.shape[0] - base) // total
    for c in range(first, rows // lanes):
        at = base + (c - first) * total
        send_ref[at : at + total, :] = ints[:, c * lanes : (c + 1) * lanes]


def direct_kernel(sizes, *refs):
    vir_parts, vir_own, occ_own, high, deep, width = sizes
    got_ref, occ_ref, vir_ref, *amp_refs, lad_ref, inv_ref, sel_ref, all_ref = refs
    me = lax.axis_index("vv")
    depth = amp_refs[0].shape[0]
    for rel, ref in enumerate(amp_refs):
        at = pl.multiple_of(jnp.bitwise_xor(me, rel) * depth, depth)
        all_ref[pl.ds(at, depth), :] = ref[...]
    ints = integral_columns(got_ref, high, deep)
    lad_ref[...] = lax.dot_general(
        ints, all_ref[...], (((0,), (0,)), ((), ())), preferred_element_type=F32
    ).astype(BF16)
    rows, cols = inv_ref.shape
    vir_all, occ_all = vir_parts * vir_own, occ_ref.shape[1]
    occ = occ_ref[...]
    occ_column = pick_sum(occ, square_eye(occ_all), 1)
    mine = lax.axis_index("oo") * occ_own + columns(cols) // occ_all
    occ_mine = pick_sum(occ_column, lax.broadcasted_iota(jnp.int32, (occ_all, cols), 0) == mine, 0)
    occ_pair = occ_mine + jnp.concatenate([occ] * occ_own, axis=1)
    lane = lax.broadcasted_iota(jnp.int32, (rows, vir_all), 1)
    row = lax.broadcasted_iota(jnp.int32, (rows, 1), 0)
    vir = vir_ref[...]
    vir_mine = pick_sum(vir, lane == me * vir_own + row // vir_all, 1)
    vir_other = pick_sum(vir, lane == row % vir_all, 1)
    inv_ref[...] = 1.0 / (occ_pair - vir_mine - vir_other)
    n, area = sel_ref.shape[1], vir_own * vir_own
    rel = jnp.bitwise_xor(row % vir_all // vir_own, me)
    source = rel * width + (rel % (width // area)) * area + row // vir_all * vir_own + row % vir_own
    pick = lax.broadcasted_iota(jnp.int32, (rows, n), 1) == source
    sel_ref[...] = jnp.where(pick, 1.0, 0.0).astype(BF16)


def choose_kernel(own, source_ref):
    cols = source_ref.shape[1]
    square, occ_all = own * own, cols // own
    col = columns(cols)
    source_ref[...] = (col % square // own) * occ_all + (col // square) * own + col % own


def mirror_kernel(sizes, *refs):
    depth, total, width = sizes
    lad_ref, inv_ref, sel_ref, *got_refs, out_hbm, all_ref, out_ref, sems = refs
    me = lax.axis_index("vv")
    rows, cols = out_ref.shape
    chunks = cols // LANES
    for rel, ref in enumerate(got_refs):
        at = pl.multiple_of(jnp.bitwise_xor(me, rel) * depth, depth)
        for c in range(chunks):
            all_ref[pl.ds(at, depth), c * LANES : (c + 1) * LANES] = ref[c * depth : (c + 1) * depth, :]
    base = chunks * depth
    ints = jnp.concatenate(
        [
            ref[base + c * total : base + (c + 1) * total, :]
            for ref in got_refs
            for c in range(width // LANES)
        ],
        axis=1,
    )
    rows_mirrored = lax.dot_general(
        sel_ref[...], ints, (((1,), (1,)), ((), ())), preferred_element_type=F32
    ).astype(BF16)
    pieces = sems.shape[0]
    size = rows // pieces
    stores = []
    for piece in range(pieces):
        some = slice(piece * size, (piece + 1) * size)
        mirrored = jnp.dot(rows_mirrored[some], all_ref[...], preferred_element_type=F32)
        both = lad_ref[some, :].astype(F32) + mirrored.astype(BF16).astype(F32)
        out_ref[some, :] = (both * inv_ref[some, :]).astype(BF16)
        stores.append(
            pltpu.make_async_copy(out_ref.at[some, :], out_hbm.at[some, :], sems.at[piece])
        )
        stores[-1].start()
    for store in stores:
        store.wait()


def call(kernel, outs, args, scratch=(), flops=0, out_space=VMEM):
    outs = tuple(outs)
    moved = sum(x.size * x.dtype.itemsize for x in (*args, *outs))
    result = pl.pallas_call(
        kernel,
        out_shape=outs,
        in_specs=[pl.BlockSpec(memory_space=VMEM)] * len(args),
        out_specs=tuple(pl.BlockSpec(memory_space=out_space) for _ in outs),
        scratch_shapes=list(scratch),
        compiler_params=pltpu.CompilerParams(vmem_limit_bytes=min(MOST, LEAST + 3 * moved)),
        cost_estimate=pl.CostEstimate(flops=flops, bytes_accessed=moved, transcendentals=0),
    )(*args)
    return result


def on_device(integrals, amplitudes, occ_energy, vir_energy):
    vir_parts, occ_parts = lax.axis_size("vv"), lax.axis_size("oo")
    vir_all, occ_all = vir_energy.shape[0], occ_energy.shape[0]
    vir_own, occ_own = vir_all // vir_parts, occ_all // occ_parts
    depth, cols = amplitudes.shape
    rows, deep = integrals.shape
    total = deep * occ_parts
    high = depth * occ_own * occ_own // LANES
    area = vir_own * vir_own

    def swap(x, step):
        return lax.ppermute(x, "vv", [(k, k ^ step) for k in range(vir_parts)])

    steps = [1 << bit for bit in reversed(range((vir_parts - 1).bit_length()))]
    widths = [s * area for s in steps if s * area % LANES == 0] or [rows]
    width = widths[-1]

    (source,) = call(
        functools.partial(choose_kernel, occ_own),
        [jax.ShapeDtypeStruct((1, cols), jnp.int32)],
        (),
        flops=CHOOSE_FLOPS,
    )

    shape = (occ_parts, high + rows // LANES * deep, LANES)
    (packed,) = call(
        functools.partial(pack_kernel, occ_own),
        [jax.ShapeDtypeStruct(shape, BF16)],
        (amplitudes, integrals.T, source),
        flops=2 * depth * cols * cols,
    )
    got = lax.all_to_all(packed, "oo", 0, 0, tiled=True, axis_index_groups=[middle_out(occ_parts)])

    amp_rows = cols // LANES * depth
    send_shape = jax.ShapeDtypeStruct((amp_rows + widths[0] // LANES * total, LANES), BF16)
    send, keep = call(
        functools.partial(
            split_kernel, (vir_parts, vir_own, occ_own, high, deep, widths[0] // LANES)
        ),
        [send_shape] * 2,
        (got,),
        flops=2 * depth * cols * cols + 2 * total * rows * rows,
    )
    held = {0: (send, keep)}
    direct = {0: amplitudes}
    for at, step in enumerate(steps):
        direct |= {k ^ step: swap(x, step) for k, x in direct.items()}
        arrived = {k: x for k, (_, x) in held.items()}
        arrived |= {k ^ step: swap(x, step) for k, (x, _) in held.items()}
        if at + 1 < len(widths):
            cut = amp_rows + widths[at + 1] // LANES * total
            held = {
                k: (jnp.concatenate([x[:amp_rows], x[cut:]]), x[:cut]) for k, x in arrived.items()
            }
        else:
            held = {k: (x, x) for k, x in arrived.items()}
    order = range(vir_parts)

    ladder, inverse, to_rows = call(
        functools.partial(direct_kernel, (vir_parts, vir_own, occ_own, high, deep, width)),
        [
            jax.ShapeDtypeStruct((rows, cols), BF16),
            jax.ShapeDtypeStruct((rows, cols), F32),
            jax.ShapeDtypeStruct((rows, vir_parts * width), BF16),
        ],
        (
            got,
            occ_energy.reshape(1, occ_all),
            vir_energy.reshape(1, vir_all),
            *(direct[k] for k in order),
        ),
        scratch=[pltpu.VMEM((total, cols), BF16)],
        flops=2 * rows * total * cols,
    )
    (update,) = call(
        functools.partial(mirror_kernel, (depth, total, width)),
        [jax.ShapeDtypeStruct((rows, cols), BF16)],
        (ladder, inverse, to_rows, *(arrived[k] for k in order)),
        scratch=[
            pltpu.VMEM((total, cols), BF16),
            pltpu.VMEM((rows, cols), BF16),
            pltpu.SemaphoreType.DMA((STORES,)),
        ],
        flops=2 * rows * total * cols * 2,
        out_space=pl.ANY,
    )
    return update


def solution(mesh):
    placed = (P("vv", "oo"), P("vv", "oo"), P(), P())
    return jax.shard_map(
        on_device, mesh=mesh, in_specs=placed, out_specs=P("vv", "oo"), check_vma=False
    )
```

```python
import functools

import jax
import jax.numpy as jnp
from jax import lax
from jax.experimental import pallas as pl
from jax.experimental.pallas import tpu as pltpu
from jax.sharding import PartitionSpec as P


LANES, STORES = 128, 2
LEAST, MOST = 8 << 20, 60 << 20
CHOOSE_FLOPS = 10**9
F32 = jnp.float32
BF16 = jnp.bfloat16
VMEM = pltpu.MemorySpace.VMEM


def one_hot(rows, source):
    n = source.shape[1]
    pick = lax.broadcasted_iota(jnp.int32, (rows, n), 0) == source
    return jnp.where(pick, 1.0, 0.0).astype(BF16)


def middle_out(n):
    half, chunk = n // 2, max(1, n // 4)
    up, down = list(range(half, n)), list(reversed(range(half)))
    order = []
    for at in range(0, max(len(up), len(down)), chunk):
        order += sorted(up[at : at + chunk], reverse=at > 0) + down[at : at + chunk]
    return order


def places(n):
    order = middle_out(n)
    return [order.index(k) for k in range(n)]


def columns(n):
    return lax.broadcasted_iota(jnp.int32, (1, n), 1)


def square_eye(n):
    return lax.broadcasted_iota(jnp.int32, (n, n), 0) == lax.broadcasted_iota(jnp.int32, (n, n), 1)


def pick_sum(values, where, axis):
    return jnp.sum(jnp.where(where, values, 0.0), axis=axis, keepdims=True)


def pack_kernel(own, t_ref, v_ref, source_ref, out_ref):
    parts, rows, lanes = out_ref.shape
    depth, cols = t_ref.shape
    square = own * own
    moved = jnp.dot(t_ref[...], one_hot(cols, source_ref[...]), preferred_element_type=F32)
    fold = lanes // square
    high = depth // fold
    for at, part in enumerate(middle_out(parts)):
        piece = [
            moved[h * high : (h + 1) * high, part * square : (part + 1) * square]
            for h in range(fold)
        ]
        out_ref[at, :high, :] = jnp.concatenate(piece, axis=1).astype(BF16)
    deep = v_ref.shape[0]
    for chunk in range((rows - high) // deep):
        block = v_ref[:, chunk * lanes : (chunk + 1) * lanes]
        for part in range(parts):
            out_ref[part, high + chunk * deep : high + (chunk + 1) * deep, :] = block


def integral_columns(got_ref, high, deep):
    parts, rows, _ = got_ref.shape
    return jnp.concatenate(
        [
            jnp.concatenate(
                [got_ref[at, high + c * deep : high + (c + 1) * deep, :] for at in places(parts)],
                axis=0,
            )
            for c in range((rows - high) // deep)
        ],
        axis=1,
    )


def split_kernel(occ_own, high, deep, got_ref, amp_ref, int_ref, send_ref, keep_ref):
    parts, _, lanes = got_ref.shape
    square = occ_own * occ_own
    cols = parts * square
    packed = got_ref[:, :high, :].astype(F32)
    halves = [
        jnp.concatenate(
            [packed[at, :, h * square : (h + 1) * square] for at in places(parts)], axis=1
        )
        for h in range(lanes // square)
    ]
    amps = jnp.concatenate(halves, axis=0).astype(BF16)
    amps = jnp.dot(amps, amp_ref[...], preferred_element_type=F32).astype(BF16)
    ints = integral_columns(got_ref, high, deep)
    total, rows = ints.shape
    ints = jnp.dot(ints, int_ref[...], preferred_element_type=F32).astype(BF16)
    depth = amps.shape[0]
    base = cols // lanes * depth
    kept = (send_ref.shape[0] - base) // total
    for ref, first in ((send_ref, rows // lanes - kept), (keep_ref, 0)):
        for c in range(cols // lanes):
            ref[c * depth : (c + 1) * depth, :] = amps[:, c * lanes : (c + 1) * lanes]
        for c in range(kept):
            at = (first + c) * lanes
            ref[base + c * total : base + (c + 1) * total, :] = ints[:, at : at + lanes]


def prepare_kernel(sizes, occ_ref, vir_ref, amp_ref, int_ref, sel_ref, inv_ref):
    vir_parts, vir_own, occ_own, width = sizes
    rows, cols = inv_ref.shape
    vir_all, occ_all = vir_parts * vir_own, occ_ref.shape[1]
    square, area = occ_own * occ_own, vir_own * vir_own
    me = lax.axis_index("vv")
    col = columns(cols)
    source = (col % occ_all // occ_own) * square + (col % occ_own) * occ_own + col // occ_all
    amp_ref[...] = one_hot(cols, source)
    col = columns(rows)
    owner = jnp.bitwise_xor(col // area, me)
    source = (col % vir_own) * vir_all + owner * vir_own + col % area // vir_own
    int_ref[...] = one_hot(rows, source)
    row = lax.broadcasted_iota(jnp.int32, (rows, 1), 0)
    rel = jnp.bitwise_xor(row % vir_all // vir_own, me)
    source = rel * width + (rel % (width // area)) * area + row // vir_all * vir_own + row % vir_own
    pick = lax.broadcasted_iota(jnp.int32, sel_ref.shape, 1) == source
    sel_ref[...] = jnp.where(pick, 1.0, 0.0).astype(BF16)
    occ = occ_ref[...]
    occ_column = pick_sum(occ, square_eye(occ_all), 1)
    mine = lax.axis_index("oo") * occ_own + columns(cols) // occ_all
    occ_mine = pick_sum(occ_column, lax.broadcasted_iota(jnp.int32, (occ_all, cols), 0) == mine, 0)
    occ_pair = occ_mine + jnp.concatenate([occ] * occ_own, axis=1)
    lane = lax.broadcasted_iota(jnp.int32, (rows, vir_all), 1)
    vir = vir_ref[...]
    vir_mine = pick_sum(vir, lane == me * vir_own + row // vir_all, 1)
    vir_other = pick_sum(vir, lane == row % vir_all, 1)
    inv_ref[...] = 1.0 / (occ_pair - vir_mine - vir_other)


def direct_kernel(high, deep, got_ref, *refs):
    *amp_refs, lad_ref, all_ref = refs
    me = lax.axis_index("vv")
    depth = amp_refs[0].shape[0]
    for rel, ref in enumerate(amp_refs):
        at = pl.multiple_of(jnp.bitwise_xor(me, rel) * depth, depth)
        all_ref[pl.ds(at, depth), :] = ref[...]
    ints = integral_columns(got_ref, high, deep)
    lad_ref[...] = lax.dot_general(
        ints, all_ref[...], (((0,), (0,)), ((), ())), preferred_element_type=F32
    ).astype(BF16)


def choose_kernel(own, source_ref):
    cols = source_ref.shape[1]
    square, occ_all = own * own, cols // own
    col = columns(cols)
    source_ref[...] = (col % square // own) * occ_all + (col // square) * own + col % own


def mirror_kernel(depth, *refs):
    lad_ref, inv_ref, sel_ref, *got_refs, out_hbm, all_ref, out_ref, sems = refs
    me = lax.axis_index("vv")
    rows, cols = out_ref.shape
    total = all_ref.shape[0]
    chunks = cols // LANES
    for rel, ref in enumerate(got_refs):
        at = pl.multiple_of(jnp.bitwise_xor(me, rel) * depth, depth)
        for c in range(chunks):
            all_ref[pl.ds(at, depth), c * LANES : (c + 1) * LANES] = ref[c * depth : (c + 1) * depth, :]
    base = chunks * depth
    ints = jnp.concatenate(
        [
            ref[at : at + total, :]
            for ref in got_refs
            for at in range(base, ref.shape[0], total)
        ],
        axis=1,
    )
    rows_mirrored = lax.dot_general(
        sel_ref[...], ints, (((1,), (1,)), ((), ())), preferred_element_type=F32
    ).astype(BF16)
    pieces = sems.shape[0]
    size = rows // pieces
    stores = []
    for piece in range(pieces):
        some = slice(piece * size, (piece + 1) * size)
        mirrored = jnp.dot(rows_mirrored[some], all_ref[...], preferred_element_type=F32)
        both = lad_ref[some, :].astype(F32) + mirrored.astype(BF16).astype(F32)
        out_ref[some, :] = (both * inv_ref[some, :]).astype(BF16)
        stores.append(
            pltpu.make_async_copy(out_ref.at[some, :], out_hbm.at[some, :], sems.at[piece])
        )
        stores[-1].start()
    for store in stores:
        store.wait()


def call(kernel, outs, args, scratch=(), flops=0, out_space=VMEM):
    outs = tuple(outs)
    moved = sum(x.size * x.dtype.itemsize for x in (*args, *outs))
    result = pl.pallas_call(
        kernel,
        out_shape=outs,
        in_specs=[pl.BlockSpec(memory_space=VMEM)] * len(args),
        out_specs=tuple(pl.BlockSpec(memory_space=out_space) for _ in outs),
        scratch_shapes=list(scratch),
        compiler_params=pltpu.CompilerParams(vmem_limit_bytes=min(MOST, LEAST + 3 * moved)),
        cost_estimate=pl.CostEstimate(flops=flops, bytes_accessed=moved, transcendentals=0),
    )(*args)
    return result


def on_device(integrals, amplitudes, occ_energy, vir_energy):
    vir_parts, occ_parts = lax.axis_size("vv"), lax.axis_size("oo")
    vir_all, occ_all = vir_energy.shape[0], occ_energy.shape[0]
    vir_own, occ_own = vir_all // vir_parts, occ_all // occ_parts
    depth, cols = amplitudes.shape
    rows, deep = integrals.shape
    total = deep * occ_parts
    high = depth * occ_own * occ_own // LANES
    area = vir_own * vir_own

    def struct(*shape, dtype=BF16):
        return jax.ShapeDtypeStruct(shape, dtype)

    def swap(x, step):
        return lax.ppermute(x, "vv", [(k, k ^ step) for k in range(vir_parts)])

    steps = [1 << bit for bit in reversed(range((vir_parts - 1).bit_length()))]
    widths = [s * area for s in steps if s * area % LANES == 0] or [rows]
    width = widths[-1]

    (source,) = call(
        functools.partial(choose_kernel, occ_own),
        [struct(1, cols, dtype=jnp.int32)],
        (),
        flops=CHOOSE_FLOPS,
    )

    (packed,) = call(
        functools.partial(pack_kernel, occ_own),
        [struct(occ_parts, high + rows // LANES * deep, LANES)],
        (amplitudes, integrals.T, source),
        flops=2 * depth * cols * cols,
    )
    got = lax.all_to_all(packed, "oo", 0, 0, tiled=True, axis_index_groups=[middle_out(occ_parts)])
    to_amps, to_ints, to_rows, inverse = call(
        functools.partial(prepare_kernel, (vir_parts, vir_own, occ_own, width)),
        [
            struct(cols, cols),
            struct(rows, rows),
            struct(rows, vir_parts * width),
            struct(rows, cols, dtype=F32),
        ],
        (occ_energy.reshape(1, occ_all), vir_energy.reshape(1, vir_all)),
    )

    amp_rows = cols // LANES * depth
    send, keep = call(
        functools.partial(split_kernel, occ_own, high, deep),
        [struct(amp_rows + widths[0] // LANES * total, LANES)] * 2,
        (got, to_amps, to_ints),
        flops=2 * depth * cols * cols + 2 * total * rows * rows,
    )
    held = {0: (send, keep)}
    direct = {0: amplitudes}
    for at, step in enumerate(steps):
        direct |= {k ^ step: swap(x, step) for k, x in direct.items()}
        arrived = {k: x for k, (_, x) in held.items()}
        arrived |= {k ^ step: swap(x, step) for k, (x, _) in held.items()}
        if at + 1 < len(widths):
            cut = amp_rows + widths[at + 1] // LANES * total
            held = {
                k: (jnp.concatenate([x[:amp_rows], x[cut:]]), x[:cut]) for k, x in arrived.items()
            }
        else:
            held = {k: (x, x) for k, x in arrived.items()}
    order = range(vir_parts)

    (ladder,) = call(
        functools.partial(direct_kernel, high, deep),
        [struct(rows, cols)],
        (got, *(direct[k] for k in order)),
        scratch=[pltpu.VMEM((total, cols), BF16)],
        flops=2 * rows * total * cols,
    )
    (update,) = call(
        functools.partial(mirror_kernel, depth),
        [struct(rows, cols)],
        (ladder, inverse, to_rows, *(arrived[k] for k in order)),
        scratch=[
            pltpu.VMEM((total, cols), BF16),
            pltpu.VMEM((rows, cols), BF16),
            pltpu.SemaphoreType.DMA((STORES,)),
        ],
        flops=2 * rows * total * cols * 2,
        out_space=pl.ANY,
    )
    return update


def solution(mesh):
    placed = (P("vv", "oo"), P("vv", "oo"), P(), P())
    return jax.shard_map(
        on_device, mesh=mesh, in_specs=placed, out_specs=P("vv", "oo"), check_vma=False
    )
```

```python
import functools

import jax
import jax.numpy as jnp
from jax import lax
from jax.experimental import pallas as pl
from jax.experimental.pallas import tpu as pltpu
from jax.sharding import PartitionSpec as P


LANES = 128
LEAST, MOST = 8 << 20, 60 << 20
CHOOSE_FLOPS = 10**9
F32 = jnp.float32
BF16 = jnp.bfloat16
VMEM = pltpu.MemorySpace.VMEM


def one_hot(rows, source):
    n = source.shape[1]
    pick = lax.broadcasted_iota(jnp.int32, (rows, n), 0) == source
    return jnp.where(pick, 1.0, 0.0).astype(BF16)


def one_hot_rows(source, n):
    pick = lax.broadcasted_iota(jnp.int32, (source.shape[0], n), 1) == source
    return jnp.where(pick, 1.0, 0.0).astype(BF16)


def choose_rows(order, columns_first):
    return lax.dot_general(
        order, columns_first, (((1,), (1,)), ((), ())), preferred_element_type=F32
    ).astype(BF16)


def middle_out(n):
    half, chunk = n // 2, max(1, n // 4)
    up, down = list(range(half, n)), list(reversed(range(half)))
    order = []
    for at in range(0, max(len(up), len(down)), chunk):
        order += sorted(up[at : at + chunk], reverse=at > 0) + down[at : at + chunk]
    return order


def places(n):
    order = middle_out(n)
    return [order.index(k) for k in range(n)]


def columns(n):
    return lax.broadcasted_iota(jnp.int32, (1, n), 1)


def square_eye(n):
    return lax.broadcasted_iota(jnp.int32, (n, n), 0) == lax.broadcasted_iota(jnp.int32, (n, n), 1)


def pick_sum(values, where, axis):
    return jnp.sum(jnp.where(where, values, 0.0), axis=axis, keepdims=True)


def pack_kernel(own, t_ref, v_ref, source_ref, out_ref):
    parts, rows, lanes = out_ref.shape
    depth, cols = t_ref.shape
    square = own * own
    moved = jnp.dot(t_ref[...], one_hot(cols, source_ref[...]), preferred_element_type=F32)
    fold = lanes // square
    high = depth // fold
    for at, part in enumerate(middle_out(parts)):
        piece = [
            moved[h * high : (h + 1) * high, part * square : (part + 1) * square]
            for h in range(fold)
        ]
        out_ref[at, :high, :] = jnp.concatenate(piece, axis=1).astype(BF16)
    deep = v_ref.shape[0]
    for chunk in range((rows - high) // deep):
        block = v_ref[:, chunk * lanes : (chunk + 1) * lanes]
        for part in range(parts):
            out_ref[part, high + chunk * deep : high + (chunk + 1) * deep, :] = block


def integral_columns(got_ref, high, deep):
    parts, rows, _ = got_ref.shape
    return jnp.concatenate(
        [
            jnp.concatenate(
                [got_ref[at, high + c * deep : high + (c + 1) * deep, :] for at in places(parts)],
                axis=0,
            )
            for c in range((rows - high) // deep)
        ],
        axis=1,
    )


def split_kernel(vir_parts, occ_own, high, deep, got_ref, amp_ref, int_ref, send_ref, keep_ref):
    parts, _, lanes = got_ref.shape
    square = occ_own * occ_own
    cols = parts * square
    packed = got_ref[:, :high, :].astype(F32)
    halves = [
        jnp.concatenate(
            [packed[at, :, h * square : (h + 1) * square] for at in places(parts)], axis=1
        )
        for h in range(lanes // square)
    ]
    amps = jnp.concatenate(halves, axis=0).astype(BF16)
    amps = jnp.dot(amps, amp_ref[...], preferred_element_type=F32).astype(BF16)
    ints = choose_rows(int_ref[...], integral_columns(got_ref, high, deep))
    depth = amps.shape[0]
    base = cols // lanes * depth
    rows, total = ints.shape
    area = rows // vir_parts
    kept = (send_ref.shape[0] - base) // (area * (total // lanes))
    for ref, first in ((send_ref, vir_parts - kept), (keep_ref, 0)):
        for c in range(cols // lanes):
            ref[c * depth : (c + 1) * depth, :] = amps[:, c * lanes : (c + 1) * lanes]
        at = base
        for rel in range(first, first + kept):
            for c in range(total // lanes):
                ref[at : at + area, :] = ints[
                    rel * area : (rel + 1) * area, c * lanes : (c + 1) * lanes
                ]
                at += area


def prepare_kernel(sizes, occ_ref, vir_ref, amp_ref, int_ref, row_ref, inv_ref):
    vir_parts, vir_own, occ_own = sizes
    rows, cols = inv_ref.shape
    vir_all, occ_all = vir_parts * vir_own, occ_ref.shape[1]
    square, area = occ_own * occ_own, vir_own * vir_own
    me = lax.axis_index("vv")
    col = columns(cols)
    source = (col % occ_all // occ_own) * square + (col % occ_own) * occ_own + col // occ_all
    amp_ref[...] = one_hot(cols, source)
    row = lax.broadcasted_iota(jnp.int32, (rows, 1), 0)
    other = jnp.bitwise_xor(row // area, me) * vir_own
    outer, inner = row % area // vir_own, row % vir_own
    int_ref[...] = one_hot_rows(inner * vir_all + other + outer, rows)
    row_ref[...] = one_hot_rows(outer * vir_all + other + inner, rows)
    occ = occ_ref[...]
    occ_column = pick_sum(occ, square_eye(occ_all), 1)
    mine = lax.axis_index("oo") * occ_own + columns(cols) // occ_all
    occ_mine = pick_sum(occ_column, lax.broadcasted_iota(jnp.int32, (occ_all, cols), 0) == mine, 0)
    occ_pair = occ_mine + jnp.concatenate([occ] * occ_own, axis=1)
    lane = lax.broadcasted_iota(jnp.int32, (rows, vir_all), 1)
    vir = vir_ref[...]
    vir_mine = pick_sum(vir, lane == me * vir_own + outer, 1)
    vir_other = pick_sum(vir, lane == other + inner, 1)
    inv_ref[...] = 1.0 / (occ_pair - vir_mine - vir_other)


def direct_kernel(high, deep, got_ref, row_ref, *refs):
    *amp_refs, lad_ref, all_ref = refs
    me = lax.axis_index("vv")
    depth = amp_refs[0].shape[0]
    for rel, ref in enumerate(amp_refs):
        at = pl.multiple_of(jnp.bitwise_xor(me, rel) * depth, depth)
        all_ref[pl.ds(at, depth), :] = ref[...]
    ints = choose_rows(row_ref[...], integral_columns(got_ref, high, deep))
    ladder = jnp.dot(ints, all_ref[...], preferred_element_type=F32)
    lad_ref[...] = ladder.astype(BF16)


def choose_kernel(own, source_ref):
    cols = source_ref.shape[1]
    square, occ_all = own * own, cols // own
    col = columns(cols)
    source_ref[...] = (col % square // own) * occ_all + (col // square) * own + col % own


def mirror_kernel(depth, *refs):
    lad_ref, inv_ref, *got_refs, out_hbm, all_ref, out_ref, sems = refs
    me = lax.axis_index("vv")
    _, own, _, cols = out_ref.shape
    total = all_ref.shape[0]
    area = own * own
    chunks = cols // LANES
    for rel, ref in enumerate(got_refs):
        at = pl.multiple_of(jnp.bitwise_xor(me, rel) * depth, depth)
        for c in range(chunks):
            all_ref[pl.ds(at, depth), c * LANES : (c + 1) * LANES] = ref[c * depth : (c + 1) * depth, :]
    base = chunks * depth
    stores = []
    for rel, ref in enumerate(got_refs):
        first = base + (rel % 2) * area * (total // LANES)
        ints = jnp.concatenate(
            [
                ref[first + c * area : first + (c + 1) * area, :]
                for c in range(total // LANES)
            ],
            axis=1,
        )
        mirrored = jnp.dot(ints, all_ref[...], preferred_element_type=F32)
        some = slice(rel * area, (rel + 1) * area)
        both = lad_ref[some, :].astype(F32) + mirrored.astype(BF16).astype(F32)
        both = both * inv_ref[some, :]
        out_ref[rel] = both.reshape(own, own, cols).astype(BF16)
        other = jnp.bitwise_xor(me, rel)
        stores.append(
            pltpu.make_async_copy(out_ref.at[rel], out_hbm.at[:, other], sems.at[rel])
        )
        stores[-1].start()
    for store in stores:
        store.wait()


def call(kernel, outs, args, scratch=(), flops=0, out_space=VMEM):
    outs = tuple(outs)
    moved = sum(x.size * x.dtype.itemsize for x in (*args, *outs))
    result = pl.pallas_call(
        kernel,
        out_shape=outs,
        in_specs=[pl.BlockSpec(memory_space=VMEM)] * len(args),
        out_specs=tuple(pl.BlockSpec(memory_space=out_space) for _ in outs),
        scratch_shapes=list(scratch),
        compiler_params=pltpu.CompilerParams(vmem_limit_bytes=min(MOST, LEAST + 3 * moved)),
        cost_estimate=pl.CostEstimate(flops=flops, bytes_accessed=moved, transcendentals=0),
    )(*args)
    return result


def on_device(integrals, amplitudes, occ_energy, vir_energy):
    vir_parts, occ_parts = lax.axis_size("vv"), lax.axis_size("oo")
    vir_all, occ_all = vir_energy.shape[0], occ_energy.shape[0]
    vir_own, occ_own = vir_all // vir_parts, occ_all // occ_parts
    depth, cols = amplitudes.shape
    rows, deep = integrals.shape
    total = deep * occ_parts
    high = depth * occ_own * occ_own // LANES
    area = vir_own * vir_own

    def struct(*shape, dtype=BF16):
        return jax.ShapeDtypeStruct(shape, dtype)

    def swap(x, step):
        return lax.ppermute(x, "vv", [(k, k ^ step) for k in range(vir_parts)])

    steps = [1 << bit for bit in reversed(range((vir_parts - 1).bit_length()))]

    (source,) = call(
        functools.partial(choose_kernel, occ_own),
        [struct(1, cols, dtype=jnp.int32)],
        (),
        flops=CHOOSE_FLOPS,
    )

    (packed,) = call(
        functools.partial(pack_kernel, occ_own),
        [struct(occ_parts, high + rows // LANES * deep, LANES)],
        (amplitudes, integrals.T, source),
        flops=2 * depth * cols * cols,
    )
    got = lax.all_to_all(packed, "oo", 0, 0, tiled=True, axis_index_groups=[middle_out(occ_parts)])
    to_amps, to_ints, to_rows, inverse = call(
        functools.partial(prepare_kernel, (vir_parts, vir_own, occ_own)),
        [struct(cols, cols), struct(rows, rows), struct(rows, rows), struct(rows, cols, dtype=F32)],
        (occ_energy.reshape(1, occ_all), vir_energy.reshape(1, vir_all)),
    )

    amp_rows, int_rows = cols // LANES * depth, total // LANES * area
    send, keep = call(
        functools.partial(split_kernel, vir_parts, occ_own, high, deep),
        [struct(amp_rows + vir_parts // 2 * int_rows, LANES)] * 2,
        (got, to_amps, to_ints),
        flops=2 * depth * cols * cols + 2 * total * rows * rows,
    )
    held = {0: (send, keep)}
    direct = {0: amplitudes}
    for step in steps:
        direct |= {k ^ step: swap(x, step) for k, x in direct.items()}
        arrived = {k: x for k, (_, x) in held.items()}
        arrived |= {k ^ step: swap(x, step) for k, (x, _) in held.items()}
        if step > 2:
            cut = amp_rows + step // 2 * int_rows
            held = {
                k: (jnp.concatenate([x[:amp_rows], x[cut:]]), x[:cut]) for k, x in arrived.items()
            }
        else:
            held = {k: (x, x) for k, x in arrived.items()}
    order = range(vir_parts)

    (ladder,) = call(
        functools.partial(direct_kernel, high, deep),
        [struct(rows, cols)],
        (got, to_rows, *(direct[k] for k in order)),
        scratch=[pltpu.VMEM((total, cols), BF16)],
        flops=2 * rows * total * cols,
    )
    (update,) = call(
        functools.partial(mirror_kernel, depth),
        [struct(vir_own, vir_parts, vir_own, cols)],
        (ladder, inverse, *(arrived[k] for k in order)),
        scratch=[
            pltpu.VMEM((total, cols), BF16),
            pltpu.VMEM((vir_parts, vir_own, vir_own, cols), BF16),
            pltpu.SemaphoreType.DMA((vir_parts,)),
        ],
        flops=2 * rows * total * cols * 2,
        out_space=pl.ANY,
    )
    return update.reshape(rows, cols)


def solution(mesh):
    placed = (P("vv", "oo"), P("vv", "oo"), P(), P())
    return jax.shard_map(
        on_device, mesh=mesh, in_specs=placed, out_specs=P("vv", "oo"), check_vma=False
    )
```

```python
import functools
import math

import jax
import jax.numpy as jnp
from jax import lax
from jax.experimental import pallas as pl
from jax.experimental.pallas import tpu as pltpu
from jax.sharding import PartitionSpec as P


LANES = 128
LEAST, MOST = 8 << 20, 60 << 20
CHOOSE_FLOPS = 10**9
F32 = jnp.float32
BF16 = jnp.bfloat16
VMEM = pltpu.MemorySpace.VMEM


def one_hot(rows, source):
    n = source.shape[1]
    pick = lax.broadcasted_iota(jnp.int32, (rows, n), 0) == source
    return jnp.where(pick, 1.0, 0.0).astype(BF16)


def one_hot_rows(source, n):
    pick = lax.broadcasted_iota(jnp.int32, (source.shape[0], n), 1) == source
    return jnp.where(pick, 1.0, 0.0).astype(BF16)


def choose_rows(order, columns_first):
    return lax.dot_general(
        order, columns_first, (((1,), (1,)), ((), ())), preferred_element_type=F32
    ).astype(BF16)


def middle_out(n):
    half, chunk = n // 2, max(1, n // 4)
    up, down = list(range(half, n)), list(reversed(range(half)))
    order = []
    for at in range(0, max(len(up), len(down)), chunk):
        order += list(reversed(up[at : at + chunk])) + down[at : at + chunk]
    return order


def places(n):
    order = middle_out(n)
    return [order.index(k) for k in range(n)]


def columns(n):
    return lax.broadcasted_iota(jnp.int32, (1, n), 1)


def square_eye(n):
    return lax.broadcasted_iota(jnp.int32, (n, n), 0) == lax.broadcasted_iota(jnp.int32, (n, n), 1)


def pick_sum(values, where, axis):
    return jnp.sum(jnp.where(where, values, 0.0), axis=axis, keepdims=True)


def pack_kernel(own, t_ref, v_ref, source_ref, out_ref):
    parts, rows, lanes = out_ref.shape
    depth, cols = t_ref.shape
    square = own * own
    moved = jnp.dot(t_ref[...], one_hot(cols, source_ref[...]), preferred_element_type=F32)
    fold = lanes // square
    high = depth // fold
    for at, part in enumerate(middle_out(parts)):
        piece = [
            moved[h * high : (h + 1) * high, part * square : (part + 1) * square]
            for h in range(fold)
        ]
        out_ref[at, :high, :] = jnp.concatenate(piece, axis=1).astype(BF16)
    deep = v_ref.shape[0]
    for chunk in range((rows - high) // deep):
        block = v_ref[:, chunk * lanes : (chunk + 1) * lanes]
        for part in range(parts):
            out_ref[part, high + chunk * deep : high + (chunk + 1) * deep, :] = block


def integral_columns(got_ref, high, deep):
    parts, rows, _ = got_ref.shape
    return jnp.concatenate(
        [
            jnp.concatenate(
                [got_ref[at, high + c * deep : high + (c + 1) * deep, :] for at in places(parts)],
                axis=0,
            )
            for c in range((rows - high) // deep)
        ],
        axis=1,
    )


def split_kernel(vir_parts, occ_own, high, deep, got_ref, send_ref, keep_ref):
    parts, _, lanes = got_ref.shape
    square = occ_own * occ_own
    cols = parts * square
    packed = got_ref[:, :high, :].astype(F32)
    halves = [
        jnp.concatenate(
            [packed[at, :, h * square : (h + 1) * square] for at in places(parts)], axis=1
        )
        for h in range(lanes // square)
    ]
    amps = jnp.concatenate(halves, axis=0).astype(BF16)
    col, occ_all = columns(cols), parts * occ_own
    source = (col % occ_all // occ_own) * square + (col % occ_own) * occ_own + col // occ_all
    amps = jnp.dot(amps, one_hot(cols, source), preferred_element_type=F32).astype(BF16)
    ints = integral_columns(got_ref, high, deep)
    total, rows = ints.shape
    area = rows // vir_parts
    outer, other, inner = row_parts(rows, vir_parts)
    vir_own = math.isqrt(area)
    source = inner * (vir_parts * vir_own) + other + outer
    ints = choose_rows(one_hot_rows(source, rows), ints)
    depth = amps.shape[0]
    base = cols // lanes * depth
    kept = (send_ref.shape[0] - base) // (area * (total // lanes))
    for ref, first in ((send_ref, vir_parts - kept), (keep_ref, 0)):
        for c in range(cols // lanes):
            ref[c * depth : (c + 1) * depth, :] = amps[:, c * lanes : (c + 1) * lanes]
        at = base
        for rel in range(first, first + kept):
            for c in range(total // lanes):
                ref[at : at + area, :] = ints[
                    rel * area : (rel + 1) * area, c * lanes : (c + 1) * lanes
                ]
                at += area


def row_parts(rows, vir_parts):
    area = rows // vir_parts
    own = math.isqrt(area)
    row = lax.broadcasted_iota(jnp.int32, (rows, 1), 0)
    other = jnp.bitwise_xor(row // area, lax.axis_index("vv")) * own
    return row % area // own, other, row % own


def prepare_kernel(vir_parts, occ_own, occ_ref, vir_ref, row_ref, inv_ref):
    rows, cols = inv_ref.shape
    vir_all, occ_all = vir_ref.shape[1], occ_ref.shape[1]
    outer, other, inner = row_parts(rows, vir_parts)
    row_ref[...] = one_hot_rows(outer * vir_all + other + inner, rows)
    occ = occ_ref[...]
    occ_column = pick_sum(occ, square_eye(occ_all), 1)
    mine = lax.axis_index("oo") * occ_own + columns(cols) // occ_all
    occ_mine = pick_sum(occ_column, lax.broadcasted_iota(jnp.int32, (occ_all, cols), 0) == mine, 0)
    occ_pair = occ_mine + jnp.concatenate([occ] * occ_own, axis=1)
    lane = lax.broadcasted_iota(jnp.int32, (rows, vir_all), 1)
    vir = vir_ref[...]
    mine = lax.axis_index("vv") * (vir_all // vir_parts) + outer
    vir_mine = pick_sum(vir, lane == mine, 1)
    vir_other = pick_sum(vir, lane == other + inner, 1)
    inv_ref[...] = 1.0 / (occ_pair - vir_mine - vir_other)


def direct_kernel(high, deep, got_ref, row_ref, *refs):
    *amp_refs, lad_ref, all_ref = refs
    me = lax.axis_index("vv")
    depth = amp_refs[0].shape[0]
    for rel, ref in enumerate(amp_refs):
        at = pl.multiple_of(jnp.bitwise_xor(me, rel) * depth, depth)
        all_ref[pl.ds(at, depth), :] = ref[...]
    ints = choose_rows(row_ref[...], integral_columns(got_ref, high, deep))
    ladder = jnp.dot(ints, all_ref[...], preferred_element_type=F32)
    lad_ref[...] = ladder.astype(BF16)


def choose_kernel(own, source_ref):
    cols = source_ref.shape[1]
    square, occ_all = own * own, cols // own
    col = columns(cols)
    source_ref[...] = (col % square // own) * occ_all + (col // square) * own + col % own


def mirror_kernel(depth, *refs):
    lad_ref, inv_ref, *got_refs, out_hbm, all_ref, out_ref, sems = refs
    me = lax.axis_index("vv")
    _, own, _, cols = out_ref.shape
    total = all_ref.shape[0]
    area = own * own
    chunks = cols // LANES
    for rel, ref in enumerate(got_refs):
        at = pl.multiple_of(jnp.bitwise_xor(me, rel) * depth, depth)
        for c in range(chunks):
            all_ref[pl.ds(at, depth), c * LANES : (c + 1) * LANES] = ref[c * depth : (c + 1) * depth, :]
    base = chunks * depth
    stores = []
    for rel, ref in enumerate(got_refs):
        first = base + (rel % 2) * area * (total // LANES)
        ints = jnp.concatenate(
            [
                ref[first + c * area : first + (c + 1) * area, :]
                for c in range(total // LANES)
            ],
            axis=1,
        )
        mirrored = jnp.dot(ints, all_ref[...], preferred_element_type=F32)
        some = slice(rel * area, (rel + 1) * area)
        both = lad_ref[some, :].astype(F32) + mirrored.astype(BF16).astype(F32)
        both = both * inv_ref[some, :]
        out_ref[rel] = both.reshape(own, own, cols).astype(BF16)
        other = jnp.bitwise_xor(me, rel)
        stores.append(
            pltpu.make_async_copy(out_ref.at[rel], out_hbm.at[:, other], sems.at[rel])
        )
        stores[-1].start()
    for store in stores:
        store.wait()


def call(kernel, outs, args, scratch=(), flops=0, out_space=VMEM):
    outs = tuple(outs)
    moved = sum(x.size * x.dtype.itemsize for x in (*args, *outs))
    result = pl.pallas_call(
        kernel,
        out_shape=outs,
        in_specs=[pl.BlockSpec(memory_space=VMEM)] * len(args),
        out_specs=tuple(pl.BlockSpec(memory_space=out_space) for _ in outs),
        scratch_shapes=list(scratch),
        compiler_params=pltpu.CompilerParams(vmem_limit_bytes=min(MOST, LEAST + 3 * moved)),
        cost_estimate=pl.CostEstimate(flops=flops, bytes_accessed=moved, transcendentals=0),
    )(*args)
    return result


def on_device(integrals, amplitudes, occ_energy, vir_energy):
    vir_parts, occ_parts = lax.axis_size("vv"), lax.axis_size("oo")
    vir_all, occ_all = vir_energy.shape[0], occ_energy.shape[0]
    vir_own, occ_own = vir_all // vir_parts, occ_all // occ_parts
    depth, cols = amplitudes.shape
    rows, deep = integrals.shape
    total = deep * occ_parts
    high = depth * occ_own * occ_own // LANES
    area = vir_own * vir_own

    def struct(*shape, dtype=BF16):
        return jax.ShapeDtypeStruct(shape, dtype)

    def swap(x, step):
        return lax.ppermute(x, "vv", [(k, k ^ step) for k in range(vir_parts)])

    steps = [1 << bit for bit in reversed(range((vir_parts - 1).bit_length()))]

    (source,) = call(
        functools.partial(choose_kernel, occ_own),
        [struct(1, cols, dtype=jnp.int32)],
        (),
        flops=CHOOSE_FLOPS,
    )

    (packed,) = call(
        functools.partial(pack_kernel, occ_own),
        [struct(occ_parts, high + rows // LANES * deep, LANES)],
        (amplitudes, integrals.T, source),
        flops=2 * depth * cols * cols,
    )
    got = lax.all_to_all(packed, "oo", 0, 0, tiled=True, axis_index_groups=[middle_out(occ_parts)])
    to_rows, inverse = call(
        functools.partial(prepare_kernel, vir_parts, occ_own),
        [struct(rows, rows), struct(rows, cols, dtype=F32)],
        (occ_energy.reshape(1, occ_all), vir_energy.reshape(1, vir_all)),
        flops=10 * rows * cols,
    )

    amp_rows, int_rows = cols // LANES * depth, total // LANES * area
    send, keep = call(
        functools.partial(split_kernel, vir_parts, occ_own, high, deep),
        [struct(amp_rows + vir_parts // 2 * int_rows, LANES)] * 2,
        (got,),
        flops=2 * depth * cols * cols + 2 * total * rows * rows,
    )
    held = {0: (send, keep)}
    direct = {0: amplitudes}
    for step in steps:
        direct |= {k ^ step: swap(x, step) for k, x in direct.items()}
        arrived = {k: x for k, (_, x) in held.items()}
        arrived |= {k ^ step: swap(x, step) for k, (x, _) in held.items()}
        if step > 2:
            cut = amp_rows + step // 2 * int_rows
            held = {
                k: (jnp.concatenate([x[:amp_rows], x[cut:]]), x[:cut]) for k, x in arrived.items()
            }
        else:
            held = {k: (x, x) for k, x in arrived.items()}
    order = range(vir_parts)

    (ladder,) = call(
        functools.partial(direct_kernel, high, deep),
        [struct(rows, cols)],
        (got, to_rows, *(direct[k] for k in order)),
        scratch=[pltpu.VMEM((total, cols), BF16)],
        flops=2 * rows * total * cols,
    )
    (update,) = call(
        functools.partial(mirror_kernel, depth),
        [struct(vir_own, vir_parts, vir_own, cols)],
        (ladder, inverse, *(arrived[k] for k in order)),
        scratch=[
            pltpu.VMEM((total, cols), BF16),
            pltpu.VMEM((vir_parts, vir_own, vir_own, cols), BF16),
            pltpu.SemaphoreType.DMA((vir_parts,)),
        ],
        flops=2 * rows * total * cols * 2,
        out_space=pl.ANY,
    )
    return update.reshape(rows, cols)


def solution(mesh):
    placed = (P("vv", "oo"), P("vv", "oo"), P(), P())
    return jax.shard_map(
        on_device, mesh=mesh, in_specs=placed, out_specs=P("vv", "oo"), check_vma=False
    )
```

```python
import functools
import math

import jax
import jax.numpy as jnp
from jax import lax
from jax.experimental import pallas as pl
from jax.experimental.pallas import tpu as pltpu
from jax.sharding import PartitionSpec as P


LANES = 128
LEAST, MOST = 8 << 20, 60 << 20
CHOOSE_FLOPS = 10**9
F32 = jnp.float32
BF16 = jnp.bfloat16
VMEM = pltpu.MemorySpace.VMEM


def one_hot(rows, source):
    n = source.shape[1]
    pick = lax.broadcasted_iota(jnp.int32, (rows, n), 0) == source
    return jnp.where(pick, 1.0, 0.0).astype(BF16)


def one_hot_rows(source, n):
    pick = lax.broadcasted_iota(jnp.int32, (source.shape[0], n), 1) == source
    return jnp.where(pick, 1.0, 0.0).astype(BF16)


def choose_rows(order, columns_first):
    return lax.dot_general(
        order, columns_first, (((1,), (1,)), ((), ())), preferred_element_type=F32
    ).astype(BF16)


def middle_out(n):
    half, chunk = n // 2, max(1, n // 4)
    up, down = list(range(half, n)), list(reversed(range(half)))
    order = []
    for at in range(0, max(len(up), len(down)), chunk):
        order += list(reversed(up[at : at + chunk])) + down[at : at + chunk]
    return order


def places(n):
    order = middle_out(n)
    return [order.index(k) for k in range(n)]


def columns(n):
    return lax.broadcasted_iota(jnp.int32, (1, n), 1)


def square_eye(n):
    return lax.broadcasted_iota(jnp.int32, (n, n), 0) == lax.broadcasted_iota(jnp.int32, (n, n), 1)


def pick_sum(values, where, axis):
    return jnp.sum(jnp.where(where, values, 0.0), axis=axis, keepdims=True)


def pack_kernel(own, t_ref, v_ref, source_ref, out_ref):
    parts, rows, lanes = out_ref.shape
    depth, cols = t_ref.shape
    square = own * own
    moved = jnp.dot(t_ref[...], one_hot(cols, source_ref[...]), preferred_element_type=F32)
    fold = lanes // square
    high = depth // fold
    for at, part in enumerate(middle_out(parts)):
        piece = [
            moved[h * high : (h + 1) * high, part * square : (part + 1) * square]
            for h in range(fold)
        ]
        out_ref[at, :high, :] = jnp.concatenate(piece, axis=1).astype(BF16)
    deep = v_ref.shape[0]
    for chunk in range((rows - high) // deep):
        block = v_ref[:, chunk * lanes : (chunk + 1) * lanes]
        for part in range(parts):
            out_ref[part, high + chunk * deep : high + (chunk + 1) * deep, :] = block


def integral_columns(got_ref, high, deep):
    parts, rows, _ = got_ref.shape
    return jnp.concatenate(
        [
            jnp.concatenate(
                [got_ref[at, high + c * deep : high + (c + 1) * deep, :] for at in places(parts)],
                axis=0,
            )
            for c in range((rows - high) // deep)
        ],
        axis=1,
    )


def split_kernel(vir_parts, occ_own, high, deep, got_ref, send_ref, keep_ref):
    parts, _, lanes = got_ref.shape
    square = occ_own * occ_own
    cols = parts * square
    packed = got_ref[:, :high, :]
    halves = [
        jnp.concatenate(
            [packed[at, :, h * square : (h + 1) * square] for at in places(parts)], axis=1
        )
        for h in range(lanes // square)
    ]
    amps = jnp.concatenate(halves, axis=0)
    col, occ_all = columns(cols), parts * occ_own
    source = (col % occ_all // occ_own) * square + (col % occ_own) * occ_own + col // occ_all
    amps = jnp.dot(amps, one_hot(cols, source), preferred_element_type=F32).astype(BF16)
    ints = integral_columns(got_ref, high, deep)
    total, rows = ints.shape
    area = rows // vir_parts
    outer, other, inner = row_parts(rows, vir_parts)
    vir_own = math.isqrt(area)
    source = inner * (vir_parts * vir_own) + other + outer
    ints = choose_rows(one_hot_rows(source, rows), ints)
    depth = amps.shape[0]
    base = cols // lanes * depth
    kept = (send_ref.shape[0] - base) // (area * (total // lanes))
    for ref, first in ((send_ref, vir_parts - kept), (keep_ref, 0)):
        for c in range(cols // lanes):
            ref[c * depth : (c + 1) * depth, :] = amps[:, c * lanes : (c + 1) * lanes]
        at = base
        for rel in range(first, first + kept):
            for c in range(total // lanes):
                ref[at : at + area, :] = ints[
                    rel * area : (rel + 1) * area, c * lanes : (c + 1) * lanes
                ]
                at += area


def row_parts(rows, vir_parts):
    area = rows // vir_parts
    own = math.isqrt(area)
    row = lax.broadcasted_iota(jnp.int32, (rows, 1), 0)
    other = jnp.bitwise_xor(row // area, lax.axis_index("vv")) * own
    return row % area // own, other, row % own


def prepare_kernel(vir_parts, occ_own, occ_ref, vir_ref, row_ref, inv_ref):
    rows, cols = inv_ref.shape
    vir_all, occ_all = vir_ref.shape[1], occ_ref.shape[1]
    outer, other, inner = row_parts(rows, vir_parts)
    row_ref[...] = one_hot_rows(outer * vir_all + other + inner, rows)
    occ = occ_ref[...]
    occ_column = pick_sum(occ, square_eye(occ_all), 1)
    mine = lax.axis_index("oo") * occ_own + columns(cols) // occ_all
    occ_mine = pick_sum(occ_column, lax.broadcasted_iota(jnp.int32, (occ_all, cols), 0) == mine, 0)
    occ_pair = occ_mine + jnp.concatenate([occ] * occ_own, axis=1)
    lane = lax.broadcasted_iota(jnp.int32, (rows, vir_all), 1)
    vir = vir_ref[...]
    mine = lax.axis_index("vv") * (vir_all // vir_parts) + outer
    vir_mine = pick_sum(vir, lane == mine, 1)
    vir_other = pick_sum(vir, lane == other + inner, 1)
    inv_ref[...] = 1.0 / (occ_pair - vir_mine - vir_other)


def direct_kernel(high, deep, got_ref, row_ref, *refs):
    *amp_refs, lad_ref, all_ref = refs
    me = lax.axis_index("vv")
    depth = amp_refs[0].shape[0]
    for rel, ref in enumerate(amp_refs):
        at = pl.multiple_of(jnp.bitwise_xor(me, rel) * depth, depth)
        all_ref[pl.ds(at, depth), :] = ref[...]
    ints = choose_rows(row_ref[...], integral_columns(got_ref, high, deep))
    ladder = jnp.dot(ints, all_ref[...], preferred_element_type=F32)
    lad_ref[...] = ladder.astype(BF16)


def choose_kernel(own, source_ref):
    cols = source_ref.shape[1]
    square, occ_all = own * own, cols // own
    col = columns(cols)
    source_ref[...] = (col % square // own) * occ_all + (col // square) * own + col % own


def mirror_kernel(depth, *refs):
    lad_ref, inv_ref, *got_refs, out_hbm, all_ref, out_ref, sems = refs
    me = lax.axis_index("vv")
    vir_parts, own, _, cols = out_ref.shape
    total = all_ref.shape[0]
    area = own * own
    chunks = cols // LANES
    for rel, ref in enumerate(got_refs):
        at = pl.multiple_of(jnp.bitwise_xor(me, rel) * depth, depth)
        for c in range(chunks):
            all_ref[pl.ds(at, depth), c * LANES : (c + 1) * LANES] = ref[c * depth : (c + 1) * depth, :]
    base = chunks * depth
    stores = []
    ints = []
    for rel, ref in enumerate(got_refs):
        first = base + (rel % 2) * area * (total // LANES)
        ints.append(
            jnp.concatenate(
                [
                    ref[first + c * area : first + (c + 1) * area, :]
                    for c in range(total // LANES)
                ],
                axis=1,
            )
        )
    ints = jnp.concatenate(ints, axis=0)
    product = jnp.dot(ints, all_ref[...], preferred_element_type=F32)
    for rel in range(vir_parts):
        some = slice(rel * area, (rel + 1) * area)
        both = lad_ref[some, :].astype(F32) + product[some].astype(BF16).astype(F32)
        both = both * inv_ref[some, :]
        out_ref[rel] = both.reshape(own, own, cols).astype(BF16)
        other = jnp.bitwise_xor(me, rel)
        stores.append(
            pltpu.make_async_copy(out_ref.at[rel], out_hbm.at[:, other], sems.at[rel])
        )
        stores[-1].start()
    for store in stores:
        store.wait()


def call(kernel, outs, args, scratch=(), flops=0, out_space=VMEM):
    outs = tuple(outs)
    moved = sum(x.size * x.dtype.itemsize for x in (*args, *outs))
    result = pl.pallas_call(
        kernel,
        out_shape=outs,
        in_specs=[pl.BlockSpec(memory_space=VMEM)] * len(args),
        out_specs=tuple(pl.BlockSpec(memory_space=out_space) for _ in outs),
        scratch_shapes=list(scratch),
        compiler_params=pltpu.CompilerParams(vmem_limit_bytes=min(MOST, LEAST + 3 * moved)),
        cost_estimate=pl.CostEstimate(flops=flops, bytes_accessed=moved, transcendentals=0),
    )(*args)
    return result


def on_device(integrals, amplitudes, occ_energy, vir_energy):
    vir_parts, occ_parts = lax.axis_size("vv"), lax.axis_size("oo")
    vir_all, occ_all = vir_energy.shape[0], occ_energy.shape[0]
    vir_own, occ_own = vir_all // vir_parts, occ_all // occ_parts
    depth, cols = amplitudes.shape
    rows, deep = integrals.shape
    total = deep * occ_parts
    high = depth * occ_own * occ_own // LANES
    area = vir_own * vir_own

    def struct(*shape, dtype=BF16):
        return jax.ShapeDtypeStruct(shape, dtype)

    def swap(x, step):
        return lax.ppermute(x, "vv", [(k, k ^ step) for k in range(vir_parts)])

    steps = [1 << bit for bit in reversed(range((vir_parts - 1).bit_length()))]

    (source,) = call(
        functools.partial(choose_kernel, occ_own),
        [struct(1, cols, dtype=jnp.int32)],
        (),
        flops=CHOOSE_FLOPS,
    )

    (packed,) = call(
        functools.partial(pack_kernel, occ_own),
        [struct(occ_parts, high + rows // LANES * deep, LANES)],
        (amplitudes, integrals.T, source),
        flops=2 * depth * cols * cols,
    )
    got = lax.all_to_all(packed, "oo", 0, 0, tiled=True, axis_index_groups=[middle_out(occ_parts)])
    to_rows, inverse = call(
        functools.partial(prepare_kernel, vir_parts, occ_own),
        [struct(rows, rows), struct(rows, cols, dtype=F32)],
        (occ_energy.reshape(1, occ_all), vir_energy.reshape(1, vir_all)),
        flops=10 * rows * cols,
    )

    amp_rows, int_rows = cols // LANES * depth, total // LANES * area
    send, keep = call(
        functools.partial(split_kernel, vir_parts, occ_own, high, deep),
        [struct(amp_rows + vir_parts // 2 * int_rows, LANES)] * 2,
        (got,),
        flops=2 * depth * cols * cols + 2 * total * rows * rows,
    )
    held = {0: (send, keep)}
    direct = {0: amplitudes}
    for step in steps:
        direct |= {k ^ step: swap(x, step) for k, x in direct.items()}
        arrived = {k: x for k, (_, x) in held.items()}
        arrived |= {k ^ step: swap(x, step) for k, (x, _) in held.items()}
        if step > 2:
            cut = amp_rows + step // 2 * int_rows
            held = {
                k: (jnp.concatenate([x[:amp_rows], x[cut:]]), x[:cut]) for k, x in arrived.items()
            }
        else:
            held = {k: (x, x) for k, x in arrived.items()}
    order = range(vir_parts)

    (ladder,) = call(
        functools.partial(direct_kernel, high, deep),
        [struct(rows, cols)],
        (got, to_rows, *(direct[k] for k in order)),
        scratch=[pltpu.VMEM((total, cols), BF16)],
        flops=2 * rows * total * cols,
    )
    (update,) = call(
        functools.partial(mirror_kernel, depth),
        [struct(vir_own, vir_parts, vir_own, cols)],
        (ladder, inverse, *(arrived[k] for k in order)),
        scratch=[
            pltpu.VMEM((total, cols), BF16),
            pltpu.VMEM((vir_parts, vir_own, vir_own, cols), BF16),
            pltpu.SemaphoreType.DMA((vir_parts,)),
        ],
        flops=2 * rows * total * cols * 2,
        out_space=pl.ANY,
    )
    return update.reshape(rows, cols)


def solution(mesh):
    placed = (P("vv", "oo"), P("vv", "oo"), P(), P())
    return jax.shard_map(
        on_device, mesh=mesh, in_specs=placed, out_specs=P("vv", "oo"), check_vma=False
    )
```

```python
import functools
import math

import jax
import jax.numpy as jnp
from jax import lax
from jax.experimental import pallas as pl
from jax.experimental.pallas import tpu as pltpu
from jax.sharding import PartitionSpec as P


LANES = 128
LEAST, MOST = 8 << 20, 60 << 20
CHOOSE_FLOPS = 10**9
F32 = jnp.float32
BF16 = jnp.bfloat16
VMEM = pltpu.MemorySpace.VMEM


def one_hot(rows, source):
    n = source.shape[1]
    pick = lax.broadcasted_iota(jnp.int32, (rows, n), 0) == source
    return jnp.where(pick, 1.0, 0.0).astype(BF16)


def one_hot_rows(source, n):
    pick = lax.broadcasted_iota(jnp.int32, (source.shape[0], n), 1) == source
    return jnp.where(pick, 1.0, 0.0).astype(BF16)


def choose_rows(order, columns_first):
    return lax.dot_general(
        order, columns_first, (((1,), (1,)), ((), ())), preferred_element_type=F32
    ).astype(BF16)


def middle_out(n):
    half, chunk = n // 2, max(1, n // 4)
    up, down = list(range(half, n)), list(reversed(range(half)))
    order = []
    for at in range(0, max(len(up), len(down)), chunk):
        order += list(reversed(up[at : at + chunk])) + down[at : at + chunk]
    return order


def places(n):
    order = middle_out(n)
    return [order.index(k) for k in range(n)]


def columns(n):
    return lax.broadcasted_iota(jnp.int32, (1, n), 1)


def square_eye(n):
    return lax.broadcasted_iota(jnp.int32, (n, n), 0) == lax.broadcasted_iota(jnp.int32, (n, n), 1)


def pick_sum(values, where, axis):
    return jnp.sum(jnp.where(where, values, 0.0), axis=axis, keepdims=True)


def pack_kernel(own, t_ref, v_ref, source_ref, out_ref):
    parts, rows, lanes = out_ref.shape
    depth, cols = t_ref.shape
    square = own * own
    order = one_hot(cols, source_ref[...])
    moved = jnp.dot(t_ref[...], order, preferred_element_type=F32).astype(BF16)
    fold = lanes // square
    high = depth // fold
    for at, part in enumerate(middle_out(parts)):
        piece = [
            moved[h * high : (h + 1) * high, part * square : (part + 1) * square]
            for h in range(fold)
        ]
        out_ref[at, :high, :] = jnp.concatenate(piece, axis=1)
    deep = v_ref.shape[0]
    for chunk in range((rows - high) // deep):
        block = v_ref[:, chunk * lanes : (chunk + 1) * lanes]
        for part in range(parts):
            out_ref[part, high + chunk * deep : high + (chunk + 1) * deep, :] = block


def integral_columns(got_ref, high, deep):
    parts, rows, _ = got_ref.shape
    return jnp.concatenate(
        [
            jnp.concatenate(
                [got_ref[at, high + c * deep : high + (c + 1) * deep, :] for at in places(parts)],
                axis=0,
            )
            for c in range((rows - high) // deep)
        ],
        axis=1,
    )


def split_kernel(vir_parts, occ_own, high, deep, got_ref, send_ref, keep_ref):
    parts, _, lanes = got_ref.shape
    square = occ_own * occ_own
    cols = parts * square
    packed = got_ref[:, :high, :]
    halves = [
        jnp.concatenate(
            [packed[at, :, h * square : (h + 1) * square] for at in places(parts)], axis=1
        )
        for h in range(lanes // square)
    ]
    amps = jnp.concatenate(halves, axis=0)
    col, occ_all = columns(cols), parts * occ_own
    source = (col % occ_all // occ_own) * square + (col % occ_own) * occ_own + col // occ_all
    amps = jnp.dot(amps, one_hot(cols, source), preferred_element_type=F32).astype(BF16)
    ints = integral_columns(got_ref, high, deep)
    total, rows = ints.shape
    area = rows // vir_parts
    outer, other, inner = row_parts(rows, vir_parts)
    vir_own = math.isqrt(area)
    source = inner * (vir_parts * vir_own) + other + outer
    ints = choose_rows(one_hot_rows(source, rows), ints)
    depth = amps.shape[0]
    base = cols // lanes * depth
    kept = (send_ref.shape[0] - base) // (area * (total // lanes))
    for ref, first in ((send_ref, vir_parts - kept), (keep_ref, 0)):
        for c in range(cols // lanes):
            ref[c * depth : (c + 1) * depth, :] = amps[:, c * lanes : (c + 1) * lanes]
        at = base
        for rel in range(first, first + kept):
            for c in range(total // lanes):
                ref[at : at + area, :] = ints[
                    rel * area : (rel + 1) * area, c * lanes : (c + 1) * lanes
                ]
                at += area


def row_parts(rows, vir_parts):
    area = rows // vir_parts
    own = math.isqrt(area)
    row = lax.broadcasted_iota(jnp.int32, (rows, 1), 0)
    other = jnp.bitwise_xor(row // area, lax.axis_index("vv")) * own
    return row % area // own, other, row % own


def prepare_kernel(vir_parts, occ_own, occ_ref, vir_ref, row_ref, inv_ref):
    rows, cols = inv_ref.shape
    vir_all, occ_all = vir_ref.shape[1], occ_ref.shape[1]
    outer, other, inner = row_parts(rows, vir_parts)
    row_ref[...] = one_hot_rows(outer * vir_all + other + inner, rows)
    occ = occ_ref[...]
    occ_column = pick_sum(occ, square_eye(occ_all), 1)
    mine = lax.axis_index("oo") * occ_own + columns(cols) // occ_all
    occ_mine = pick_sum(occ_column, lax.broadcasted_iota(jnp.int32, (occ_all, cols), 0) == mine, 0)
    occ_pair = occ_mine + jnp.concatenate([occ] * occ_own, axis=1)
    lane = lax.broadcasted_iota(jnp.int32, (rows, vir_all), 1)
    vir = vir_ref[...]
    mine = lax.axis_index("vv") * (vir_all // vir_parts) + outer
    vir_mine = pick_sum(vir, lane == mine, 1)
    vir_other = pick_sum(vir, lane == other + inner, 1)
    inv_ref[...] = 1.0 / (occ_pair - vir_mine - vir_other)


def direct_kernel(high, deep, got_ref, row_ref, *refs):
    *amp_refs, lad_ref, all_ref = refs
    me = lax.axis_index("vv")
    depth = amp_refs[0].shape[0]
    for rel, ref in enumerate(amp_refs):
        at = pl.multiple_of(jnp.bitwise_xor(me, rel) * depth, depth)
        all_ref[pl.ds(at, depth), :] = ref[...]
    ints = choose_rows(row_ref[...], integral_columns(got_ref, high, deep))
    ladder = jnp.dot(ints, all_ref[...], preferred_element_type=F32)
    lad_ref[...] = ladder.astype(BF16)


def choose_kernel(own, source_ref):
    cols = source_ref.shape[1]
    square, occ_all = own * own, cols // own
    col = columns(cols)
    source_ref[...] = (col % square // own) * occ_all + (col // square) * own + col % own


def mirror_kernel(depth, *refs):
    lad_ref, inv_ref, *got_refs, out_hbm, all_ref, out_ref, sems = refs
    me = lax.axis_index("vv")
    vir_parts, own, _, cols = out_ref.shape
    total = all_ref.shape[0]
    area = own * own
    chunks = cols // LANES
    for rel, ref in enumerate(got_refs):
        at = pl.multiple_of(jnp.bitwise_xor(me, rel) * depth, depth)
        for c in range(chunks):
            all_ref[pl.ds(at, depth), c * LANES : (c + 1) * LANES] = ref[c * depth : (c + 1) * depth, :]
    base = chunks * depth
    stores = []
    ints = []
    for rel, ref in enumerate(got_refs):
        first = base + (rel % 2) * area * (total // LANES)
        ints.append(
            jnp.concatenate(
                [
                    ref[first + c * area : first + (c + 1) * area, :]
                    for c in range(total // LANES)
                ],
                axis=1,
            )
        )
    ints = jnp.concatenate(ints, axis=0)
    product = jnp.dot(ints, all_ref[...], preferred_element_type=F32)
    for rel in range(vir_parts):
        some = slice(rel * area, (rel + 1) * area)
        both = lad_ref[some, :].astype(F32) + product[some].astype(BF16).astype(F32)
        both = both * inv_ref[some, :]
        out_ref[rel] = both.reshape(own, own, cols).astype(BF16)
        other = jnp.bitwise_xor(me, rel)
        stores.append(
            pltpu.make_async_copy(out_ref.at[rel], out_hbm.at[:, other], sems.at[rel])
        )
        stores[-1].start()
    for store in stores:
        store.wait()


def call(kernel, outs, args, scratch=(), flops=0, out_space=VMEM):
    outs = tuple(outs)
    moved = sum(x.size * x.dtype.itemsize for x in (*args, *outs))
    result = pl.pallas_call(
        kernel,
        out_shape=outs,
        in_specs=[pl.BlockSpec(memory_space=VMEM)] * len(args),
        out_specs=tuple(pl.BlockSpec(memory_space=out_space) for _ in outs),
        scratch_shapes=list(scratch),
        compiler_params=pltpu.CompilerParams(vmem_limit_bytes=min(MOST, LEAST + 3 * moved)),
        cost_estimate=pl.CostEstimate(flops=flops, bytes_accessed=moved, transcendentals=0),
    )(*args)
    return result


def on_device(integrals, amplitudes, occ_energy, vir_energy):
    vir_parts, occ_parts = lax.axis_size("vv"), lax.axis_size("oo")
    vir_all, occ_all = vir_energy.shape[0], occ_energy.shape[0]
    vir_own, occ_own = vir_all // vir_parts, occ_all // occ_parts
    depth, cols = amplitudes.shape
    rows, deep = integrals.shape
    total = deep * occ_parts
    high = depth * occ_own * occ_own // LANES
    area = vir_own * vir_own

    def struct(*shape, dtype=BF16):
        return jax.ShapeDtypeStruct(shape, dtype)

    def swap(x, step):
        return lax.ppermute(x, "vv", [(k, k ^ step) for k in range(vir_parts)])

    steps = [1 << bit for bit in reversed(range((vir_parts - 1).bit_length()))]

    (source,) = call(
        functools.partial(choose_kernel, occ_own),
        [struct(1, cols, dtype=jnp.int32)],
        (),
        flops=CHOOSE_FLOPS,
    )

    (packed,) = call(
        functools.partial(pack_kernel, occ_own),
        [struct(occ_parts, high + rows // LANES * deep, LANES)],
        (amplitudes, integrals.T, source),
        flops=2 * depth * cols * cols,
    )
    got = lax.all_to_all(packed, "oo", 0, 0, tiled=True, axis_index_groups=[middle_out(occ_parts)])
    to_rows, inverse = call(
        functools.partial(prepare_kernel, vir_parts, occ_own),
        [struct(rows, rows), struct(rows, cols, dtype=F32)],
        (occ_energy.reshape(1, occ_all), vir_energy.reshape(1, vir_all)),
        flops=10 * rows * cols,
    )

    amp_rows, int_rows = cols // LANES * depth, total // LANES * area
    send, keep = call(
        functools.partial(split_kernel, vir_parts, occ_own, high, deep),
        [struct(amp_rows + vir_parts // 2 * int_rows, LANES)] * 2,
        (got,),
        flops=2 * depth * cols * cols + 2 * total * rows * rows,
    )
    held = {0: (send, keep)}
    direct = {0: amplitudes}
    for step in steps:
        direct |= {k ^ step: swap(x, step) for k, x in direct.items()}
        arrived = {k: x for k, (_, x) in held.items()}
        arrived |= {k ^ step: swap(x, step) for k, (x, _) in held.items()}
        if step > 2:
            cut = amp_rows + step // 2 * int_rows
            held = {
                k: (jnp.concatenate([x[:amp_rows], x[cut:]]), x[:cut]) for k, x in arrived.items()
            }
        else:
            held = {k: (x, x) for k, x in arrived.items()}
    order = range(vir_parts)

    (ladder,) = call(
        functools.partial(direct_kernel, high, deep),
        [struct(rows, cols)],
        (got, to_rows, *(direct[k] for k in order)),
        scratch=[pltpu.VMEM((total, cols), BF16)],
        flops=2 * rows * total * cols,
    )
    (update,) = call(
        functools.partial(mirror_kernel, depth),
        [struct(vir_own, vir_parts, vir_own, cols)],
        (ladder, inverse, *(arrived[k] for k in order)),
        scratch=[
            pltpu.VMEM((total, cols), BF16),
            pltpu.VMEM((vir_parts, vir_own, vir_own, cols), BF16),
            pltpu.SemaphoreType.DMA((vir_parts,)),
        ],
        flops=2 * rows * total * cols * 2,
        out_space=pl.ANY,
    )
    return update.reshape(rows, cols)


def solution(mesh):
    placed = (P("vv", "oo"), P("vv", "oo"), P(), P())
    return jax.shard_map(
        on_device, mesh=mesh, in_specs=placed, out_specs=P("vv", "oo"), check_vma=False
    )
```
